32 devices in a mesh: lat: 4 (over z), lon: 8 (over y, x, core).
Axes of the slice: x: 2, y: 2, z: 4, core: 2. Of those that a mesh axis runs over, the one named last changes fastest.
Arguments:
- tokens: bfloat16 [48, 192, 512], P('lat', 'lon'), may hold values from -100 to 100
- fine_gain: float32 [512], replicated, may hold values from 0.5 to 1.5
- fine_qkv: bfloat16 [512, 768], replicated, may hold values from -20 to 20
- fine_proj: bfloat16 [256, 512], replicated, may hold values from -0.375 to 0.375
- merge_gain: float32 [2048], replicated, may hold values from 0.5 to 1.5
- merge_weight: bfloat16 [2048, 512], replicated, may hold values from -0.125 to 0.125
- coarse_gain: float32 [512], replicated, may hold values from 0.5 to 1.5
- coarse_qkv: bfloat16 [512, 1536], replicated, may hold values from -20 to 20
- coarse_proj: bfloat16 [512, 512], replicated, may hold values from -0.25 to 0.25
- cotangent: bfloat16 [24, 96, 512], P('lat', 'lon'), may hold values from -6 to 6
Outputs:
- output: bfloat16 [24, 96, 512], P('lat', 'lon')
- grad_tokens: bfloat16 [48, 192, 512], P('lat', 'lon')
- grad_fine_gain: float32 [512], P(('lat', 'lon'))
- grad_fine_qkv: float32 [512, 768], P(('lat', 'lon'))
- grad_fine_proj: float32 [256, 512], P(('lat', 'lon'))
- grad_merge_gain: float32 [2048], P(('lat', 'lon'))
- grad_merge_weight: float32 [2048, 512], P(('lat', 'lon'))
- grad_coarse_gain: float32 [512], P(('lat', 'lon'))
- grad_coarse_qkv: float32 [512, 1536], P(('lat', 'lon'))
- grad_coarse_proj: float32 [512, 512], P(('lat', 'lon'))
The draws below stay inside these ranges and needn't reach their ends.
All inputs are finite; a program needn't handle non-finite values.
Results may differ from the reference program's by a relative error of at most 0.028.
Values may be sent and summed in bfloat16 or wider, within the bound.
A program may use at most 128 MiB of HBM per device.

```python
import math
import jax
import jax.numpy as jnp
from jax import lax

D = 512
DC = 512
HD = 64
HF = 4
HC = 8
WLAT = 6
WLON = 12
SLAT = 3
SLON = 6
NLAT = 48
NLON = 192


def projection_draw(key, breadth, head_count):
    inner = head_count * HD
    keys_all = jax.random.split(key, 1)
    matrix = jnp.clip(jax.random.normal(keys_all[0], (breadth, 3 * inner), jnp.float32), -6.0, 6.0) * breadth ** (-0.5)
    return jnp.clip(matrix, -20.0, 20.0).astype(jnp.bfloat16)


def draw_tokens(key, part):
    keys_all = jax.random.split(jax.random.fold_in(key, 11), 3)
    row_scale = jnp.exp(jax.random.uniform(keys_all[0], (NLAT, NLON, 1), jnp.float32, 0.0, math.log(10.0)))
    channel_scale = jnp.exp(jax.random.uniform(keys_all[1], (1, 1, D), jnp.float32, -0.7, 0.7))
    base_values = jax.random.normal(keys_all[2], (NLAT, NLON, D), jnp.float32)
    return jnp.clip(base_values * row_scale * channel_scale, -100.0, 100.0).astype(jnp.bfloat16)


def draw_fine_qkv(key, part):
    return projection_draw(jax.random.fold_in(key, 23), D, HF)


def draw_coarse_qkv(key, part):
    return projection_draw(jax.random.fold_in(key, 37), DC, HC)


def level_of(stream_key, extent, shards, least, high):
    factor_of = 1.0
    for position, blocks in shards:
        heights = jax.random.uniform(jax.random.fold_in(jax.random.fold_in(stream_key, 6), position), (blocks,), jnp.float32, least / len(shards), high / len(shards))
        factor_of = factor_of * jnp.repeat(jnp.exp(heights), extent[position] // blocks).reshape((-1,) + (1,) * (len(extent) - 1 - position))
    return factor_of


def centred(own_key, shape, scale, bound, pieces=(), kind=jnp.bfloat16):
    gain = level_of(own_key, shape, pieces, -0.22, 0.18) if pieces else 1.0
    values = jax.random.normal(own_key, shape, jnp.float32) * scale * gain
    return jnp.minimum(jnp.maximum(values, -bound), bound).astype(kind)


def setup_inputs(seed: int = 0) -> dict:
    streams_of = jax.random.split(jax.random.key(seed), 11)
    tokens = draw_tokens(jax.random.fold_in(streams_of[10], 71), 0)
    fine_gain = jnp.clip(1.0 + 0.1 * jax.random.normal(streams_of[1], (D,), jnp.float32), 0.5, 1.5)
    fine_qkv = draw_fine_qkv(jax.random.fold_in(streams_of[10], 71), 0)
    fine_proj = centred(streams_of[3], (HF * HD, D), (HF * HD) ** -0.5, 0.375)
    merge_gain = jnp.clip(1.0 + 0.1 * jax.random.normal(streams_of[4], (4 * D,), jnp.float32), 0.5, 1.5)
    merge_weight = centred(streams_of[5], (4 * D, DC), (4 * D) ** -0.5, 0.125)
    coarse_gain = jnp.clip(1.0 + 0.1 * jax.random.normal(streams_of[6], (DC,), jnp.float32), 0.5, 1.5)
    coarse_qkv = draw_coarse_qkv(jax.random.fold_in(streams_of[10], 71), 0)
    coarse_proj = centred(streams_of[8], (HC * HD, DC), (HC * HD) ** -0.5, 0.25)
    cotangent = centred(streams_of[9], (NLAT // 2, NLON // 2, DC), 1.0, 6.0, ((0, 4), (1, 8)))
    return {"tokens": tokens, "fine_gain": fine_gain, "fine_qkv": fine_qkv, "fine_proj": fine_proj, "merge_gain": merge_gain, "merge_weight": merge_weight, "coarse_gain": coarse_gain, "coarse_qkv": coarse_qkv, "coarse_proj": coarse_proj, "cotangent": cotangent}


EPSILON = 1e-05

def layer_norm(values, gains):
    center = lax.optimization_barrier(jnp.mean(values, axis=-1, keepdims=True))
    shifted = values - center
    spread = lax.optimization_barrier(jnp.mean(shifted * shifted, axis=-1, keepdims=True))
    return shifted * lax.rsqrt(spread + EPSILON) * gains

def window_attention(packed, row_offset, total_rows, head_count):
    row_count, col_count = (packed.shape[0], packed.shape[1])
    head_size = packed.shape[2] // (3 * head_count)
    lat_windows = row_count // WLAT
    lon_windows = col_count // WLON
    grouped = packed.reshape(lat_windows, WLAT, lon_windows, WLON, 3, head_count, head_size)
    grouped = grouped.transpose(4, 0, 2, 5, 1, 3, 6).reshape(3, lat_windows, lon_windows, head_count, WLAT * WLON, head_size)
    queries = grouped[0].astype(jnp.float32)
    keys_all = grouped[1].astype(jnp.float32)
    values_all = grouped[2].astype(jnp.float32)
    scores = jnp.einsum('abhqd,abhkd->abhqk', queries, keys_all) * head_size ** (-0.5)
    row_index = row_offset + jnp.arange(row_count, dtype=jnp.int32)
    region = (row_index >= total_rows - SLAT).reshape(lat_windows, WLAT)
    region = jnp.broadcast_to(region[:, :, None], (lat_windows, WLAT, WLON)).reshape(lat_windows, WLAT * WLON)
    allowed = region[:, None, None, :, None] == region[:, None, None, None, :]
    scores = jnp.where(allowed, scores, -1000000000.0)
    largest = lax.optimization_barrier(jnp.max(scores, axis=-1, keepdims=True))
    exponent = jnp.exp(scores - largest)
    attn_weights = (exponent / lax.optimization_barrier(jnp.sum(exponent, axis=-1, keepdims=True))).astype(jnp.bfloat16)
    mixed_out = jnp.einsum('abhqk,abhkd->abhqd', attn_weights.astype(jnp.float32), values_all).astype(jnp.bfloat16)
    mixed_out = mixed_out.reshape(lat_windows, lon_windows, head_count, WLAT, WLON, head_size)
    return mixed_out.transpose(0, 3, 1, 4, 2, 5).reshape(row_count, col_count, head_count * head_size)

def block_forward(rolled, gains, weight_qkv, weight_proj, row_offset, total_rows, head_count):
    normed = layer_norm(rolled.astype(jnp.float32), gains).astype(jnp.bfloat16)
    packed = jnp.dot(normed, weight_qkv, preferred_element_type=jnp.float32).astype(jnp.bfloat16)
    mixed_out = window_attention(packed, row_offset, total_rows, head_count)
    added = jnp.dot(mixed_out, weight_proj, preferred_element_type=jnp.float32)
    result = (rolled.astype(jnp.float32) + added).astype(jnp.bfloat16)
    return (result, (normed, packed, mixed_out))

def block_backward(grad_out, rolled, gains, weight_qkv, weight_proj, saved, row_offset, total_rows, head_count):
    normed, packed, mixed_out = saved
    grad_mixed = lax.dot_general(grad_out, weight_proj, (((2,), (1,)), ((), ())), preferred_element_type=jnp.float32).astype(jnp.bfloat16)
    grad_proj = lax.dot_general(mixed_out, grad_out, (((0, 1), (0, 1)), ((), ())), preferred_element_type=jnp.float32)

    def attend_only(packed_in):
        return window_attention(packed_in, row_offset, total_rows, head_count)
    _, attend_back = jax.vjp(attend_only, packed)
    grad_packed = attend_back(grad_mixed)[0]
    grad_normed = lax.dot_general(grad_packed, weight_qkv, (((2,), (1,)), ((), ())), preferred_element_type=jnp.float32).astype(jnp.bfloat16)
    grad_qkv = lax.dot_general(normed, grad_packed, (((0, 1), (0, 1)), ((), ())), preferred_element_type=jnp.float32)
    _, norm_back = jax.vjp(layer_norm, rolled.astype(jnp.float32), gains)
    grad_input, grad_gain = norm_back(grad_normed.astype(jnp.float32))
    grad_rolled = (grad_out.astype(jnp.float32) + grad_input).astype(jnp.bfloat16)
    return (grad_rolled, grad_gain, grad_qkv, grad_proj)

def merge_tokens(patch_grid):
    row_count, col_count, breadth = patch_grid.shape
    reshaped = patch_grid.reshape(row_count // 2, 2, col_count // 2, 2, breadth)
    return reshaped.transpose(0, 2, 3, 1, 4).reshape(row_count // 2, col_count // 2, 4 * breadth)

def split_tokens(merged_grid):
    row_count, col_count, breadth = merged_grid.shape
    narrow = breadth // 4
    reshaped = merged_grid.reshape(row_count, col_count, 2, 2, narrow)
    return reshaped.transpose(0, 3, 1, 2, 4).reshape(2 * row_count, 2 * col_count, narrow)

def merge_forward(fine_grid, gains, weight):
    packed_grid = merge_tokens(fine_grid)
    normed = layer_norm(packed_grid.astype(jnp.float32), gains).astype(jnp.bfloat16)
    merged = jnp.dot(normed, weight, preferred_element_type=jnp.float32).astype(jnp.bfloat16)
    return (merged, (packed_grid, normed))

def merge_backward(grad_merged, saved, gains, weight):
    packed_grid, normed = saved
    grad_normed = lax.dot_general(grad_merged, weight, (((2,), (1,)), ((), ())), preferred_element_type=jnp.float32).astype(jnp.bfloat16)
    grad_weight = lax.dot_general(normed, grad_merged, (((0, 1), (0, 1)), ((), ())), preferred_element_type=jnp.float32)
    _, norm_back = jax.vjp(layer_norm, packed_grid.astype(jnp.float32), gains)
    grad_packed, grad_gain = norm_back(grad_normed.astype(jnp.float32))
    return (split_tokens(grad_packed.astype(jnp.bfloat16)), grad_gain, grad_weight)

def reference(tokens, fine_gain, fine_qkv, fine_proj, merge_gain, merge_weight, coarse_gain, coarse_qkv, coarse_proj, cotangent):
    fine_total = tokens.shape[0]
    coarse_total = fine_total // 2
    grad_scale = (tokens.shape[0] * tokens.shape[1] // 4) ** (-0.5)
    start = jnp.int32(0)
    rolled_fine = jnp.roll(tokens, (-SLAT, -SLON), axis=(0, 1))
    fine_result, fine_saved = block_forward(rolled_fine, fine_gain, fine_qkv, fine_proj, start, fine_total, HF)
    fine_grid = jnp.roll(fine_result, (SLAT, SLON), axis=(0, 1))
    merged, merge_saved = merge_forward(fine_grid, merge_gain, merge_weight)
    rolled_coarse = jnp.roll(merged, (-SLAT, -SLON), axis=(0, 1))
    coarse_result, coarse_saved = block_forward(rolled_coarse, coarse_gain, coarse_qkv, coarse_proj, start, coarse_total, HC)
    output = jnp.roll(coarse_result, (SLAT, SLON), axis=(0, 1))
    grad_coarse_out = jnp.roll(cotangent, (-SLAT, -SLON), axis=(0, 1))
    grad_rolled_coarse, coarse_gain_sum, coarse_qkv_sum, coarse_proj_sum = block_backward(grad_coarse_out, rolled_coarse, coarse_gain, coarse_qkv, coarse_proj, coarse_saved, start, coarse_total, HC)
    grad_merged = jnp.roll(grad_rolled_coarse, (SLAT, SLON), axis=(0, 1))
    grad_fine_grid, merge_gain_sum, merge_weight_sum = merge_backward(grad_merged, merge_saved, merge_gain, merge_weight)
    grad_fine_out = jnp.roll(grad_fine_grid, (-SLAT, -SLON), axis=(0, 1))
    grad_rolled_fine, fine_gain_sum, fine_qkv_sum, fine_proj_sum = block_backward(grad_fine_out, rolled_fine, fine_gain, fine_qkv, fine_proj, fine_saved, start, fine_total, HF)
    grad_tokens = jnp.roll(grad_rolled_fine, (SLAT, SLON), axis=(0, 1))
    return (output, grad_tokens, fine_gain_sum * grad_scale, fine_qkv_sum * grad_scale, fine_proj_sum * grad_scale, merge_gain_sum * grad_scale, merge_weight_sum * grad_scale, coarse_gain_sum * grad_scale, coarse_qkv_sum * grad_scale, coarse_proj_sum * grad_scale)
```

```python
import jax
import jax.numpy as jnp
from jax import lax
from jax.sharding import PartitionSpec as P

HF = 4
HC = 8
WLAT = 6
WLON = 12
SLAT = 3
SLON = 6


EPSILON = 1e-05


def layer_norm(values, gains):
    center = jnp.mean(values, axis=-1, keepdims=True)
    shifted = values - center
    spread = jnp.mean(shifted * shifted, axis=-1, keepdims=True)
    return shifted * lax.rsqrt(spread + EPSILON) * gains


def window_attention(packed, row_offset, total_rows, head_count):
    row_count, col_count = (packed.shape[0], packed.shape[1])
    head_size = packed.shape[2] // (3 * head_count)
    lat_windows = row_count // WLAT
    lon_windows = col_count // WLON
    grouped = packed.reshape(lat_windows, WLAT, lon_windows, WLON, 3, head_count, head_size)
    grouped = grouped.transpose(4, 0, 2, 5, 1, 3, 6).reshape(
        3, lat_windows, lon_windows, head_count, WLAT * WLON, head_size
    )
    queries = grouped[0].astype(jnp.float32)
    keys_all = grouped[1].astype(jnp.float32)
    values_all = grouped[2].astype(jnp.float32)
    scores = jnp.einsum("abhqd,abhkd->abhqk", queries, keys_all) * head_size ** (-0.5)
    row_index = row_offset + jnp.arange(row_count, dtype=jnp.int32)
    region = (row_index >= total_rows - SLAT).reshape(lat_windows, WLAT)
    region = jnp.broadcast_to(region[:, :, None], (lat_windows, WLAT, WLON)).reshape(
        lat_windows, WLAT * WLON
    )
    allowed = region[:, None, None, :, None] == region[:, None, None, None, :]
    scores = jnp.where(allowed, scores, -1000000000.0)
    largest = jnp.max(scores, axis=-1, keepdims=True)
    exponent = jnp.exp(scores - largest)
    attn_weights = (exponent / jnp.sum(exponent, axis=-1, keepdims=True)).astype(jnp.bfloat16)
    mixed_out = jnp.einsum(
        "abhqk,abhkd->abhqd", attn_weights.astype(jnp.float32), values_all
    ).astype(jnp.bfloat16)
    mixed_out = mixed_out.reshape(lat_windows, lon_windows, head_count, WLAT, WLON, head_size)
    return mixed_out.transpose(0, 3, 1, 4, 2, 5).reshape(
        row_count, col_count, head_count * head_size
    )


def block_forward(rolled, gains, weight_qkv, weight_proj, row_offset, total_rows, head_count):
    normed = layer_norm(rolled.astype(jnp.float32), gains).astype(jnp.bfloat16)
    packed = jnp.dot(normed, weight_qkv, preferred_element_type=jnp.float32).astype(jnp.bfloat16)
    mixed_out = window_attention(packed, row_offset, total_rows, head_count)
    added = jnp.dot(mixed_out, weight_proj, preferred_element_type=jnp.float32)
    result = (rolled.astype(jnp.float32) + added).astype(jnp.bfloat16)
    return (result, (normed, packed, mixed_out))


def block_backward(
    grad_out, rolled, gains, weight_qkv, weight_proj, saved, row_offset, total_rows, head_count
):
    normed, packed, mixed_out = saved
    grad_mixed = lax.dot_general(
        grad_out, weight_proj, (((2,), (1,)), ((), ())), preferred_element_type=jnp.float32
    ).astype(jnp.bfloat16)
    grad_proj = lax.dot_general(
        mixed_out, grad_out, (((0, 1), (0, 1)), ((), ())), preferred_element_type=jnp.float32
    )

    def attend_only(packed_in):
        return window_attention(packed_in, row_offset, total_rows, head_count)

    _, attend_back = jax.vjp(attend_only, packed)
    grad_packed = attend_back(grad_mixed)[0]
    grad_normed = lax.dot_general(
        grad_packed, weight_qkv, (((2,), (1,)), ((), ())), preferred_element_type=jnp.float32
    ).astype(jnp.bfloat16)
    grad_qkv = lax.dot_general(
        normed, grad_packed, (((0, 1), (0, 1)), ((), ())), preferred_element_type=jnp.float32
    )
    _, norm_back = jax.vjp(layer_norm, rolled.astype(jnp.float32), gains)
    grad_input, grad_gain = norm_back(grad_normed.astype(jnp.float32))
    grad_rolled = (grad_out.astype(jnp.float32) + grad_input).astype(jnp.bfloat16)
    return (grad_rolled, grad_gain, grad_qkv, grad_proj)


def merge_tokens(patch_grid):
    row_count, col_count, breadth = patch_grid.shape
    reshaped = patch_grid.reshape(row_count // 2, 2, col_count // 2, 2, breadth)
    return reshaped.transpose(0, 2, 3, 1, 4).reshape(row_count // 2, col_count // 2, 4 * breadth)


def split_tokens(merged_grid):
    row_count, col_count, breadth = merged_grid.shape
    narrow = breadth // 4
    reshaped = merged_grid.reshape(row_count, col_count, 2, 2, narrow)
    return reshaped.transpose(0, 3, 1, 2, 4).reshape(2 * row_count, 2 * col_count, narrow)


def merge_forward(fine_grid, gains, weight):
    packed_grid = merge_tokens(fine_grid)
    normed = layer_norm(packed_grid.astype(jnp.float32), gains).astype(jnp.bfloat16)
    merged = jnp.dot(normed, weight, preferred_element_type=jnp.float32).astype(jnp.bfloat16)
    return (merged, (packed_grid, normed))


def merge_backward(grad_merged, saved, gains, weight):
    packed_grid, normed = saved
    grad_normed = lax.dot_general(
        grad_merged, weight, (((2,), (1,)), ((), ())), preferred_element_type=jnp.float32
    ).astype(jnp.bfloat16)
    grad_weight = lax.dot_general(
        normed, grad_merged, (((0, 1), (0, 1)), ((), ())), preferred_element_type=jnp.float32
    )
    _, norm_back = jax.vjp(layer_norm, packed_grid.astype(jnp.float32), gains)
    grad_packed, grad_gain = norm_back(grad_normed.astype(jnp.float32))
    return (split_tokens(grad_packed.astype(jnp.bfloat16)), grad_gain, grad_weight)


def shift_pairs(lat_step, lon_step):
    lats, lons = lax.axis_size("lat"), lax.axis_size("lon")
    return [
        (a * lons + b, ((a + lat_step) % lats) * lons + (b + lon_step) % lons)
        for a in range(lats)
        for b in range(lons)
    ]


def send(value, lat_step, lon_step):
    return lax.ppermute(value, ("lat", "lon"), shift_pairs(lat_step, lon_step))


def rotate_ahead(grid):
    below = send(grid[:SLAT, SLON:], -1, 0)
    beside = send(grid[SLAT:, :SLON], 0, -1)
    corner = send(grid[:SLAT, :SLON], -1, -1)
    top = jnp.concatenate([grid[SLAT:, SLON:], beside], axis=1)
    return jnp.concatenate([top, jnp.concatenate([below, corner], axis=1)], axis=0)


def rotate_back(grid):
    above = send(grid[-SLAT:, :-SLON], 1, 0)
    beside = send(grid[:-SLAT, -SLON:], 0, 1)
    corner = send(grid[-SLAT:, -SLON:], 1, 1)
    low = jnp.concatenate([beside, grid[:-SLAT, :-SLON]], axis=1)
    return jnp.concatenate([jnp.concatenate([corner, above], axis=1), low], axis=0)


def halve(value, axis, step):
    count = lax.axis_size(axis)
    bit = (lax.axis_index(axis) // step) % 2
    kept = lax.dynamic_index_in_dim(value, bit, 1, keepdims=False)
    gone = lax.dynamic_index_in_dim(value, 1 - bit, 1, keepdims=False)
    came = lax.ppermute(gone, axis, [(i, i ^ step) for i in range(count)])
    return (kept.astype(jnp.float32) + came.astype(jnp.float32)).astype(value.dtype)


def reduce_pieces(value):
    lats, lons = lax.axis_size("lat"), lax.axis_size("lon")
    rows, columns = value.shape[1:]
    if lats & (lats - 1) or lons & (lons - 1):
        total = lax.psum_scatter(value, ("lat", "lon"), scatter_dimension=0, tiled=True)
        return total.reshape(rows, columns)
    step = 1
    while step < lons:
        left = lons // step
        value = value.reshape(lats * left // 2, 2, rows, columns)
        value = halve(value, "lon", step)
        step *= 2
    step = 1
    while step < lats:
        left = lats // step
        value = value.reshape(left // 2, 2, rows, columns)
        value = halve(value, "lat", step)
        step *= 2
    return value.reshape(rows, columns)


def as_pieces(value, devices, width):
    rows = value.shape[0] // devices
    value = value.astype(jnp.bfloat16).reshape(devices, rows, value.shape[1])
    parts = [value[:, :, i : i + width] for i in range(0, value.shape[2], width)]
    return jnp.concatenate(parts, axis=1)


def from_pieces(value, rows, columns):
    width = value.shape[1]
    parts = [value[i * rows : (i + 1) * rows] for i in range(columns // width)]
    return jnp.concatenate(parts, axis=1).astype(jnp.float32)


def local(
    tokens,
    fine_gain,
    fine_qkv,
    fine_proj,
    merge_gain,
    merge_weight,
    coarse_gain,
    coarse_qkv,
    coarse_proj,
    cotangent,
):
    fine_rows = tokens.shape[0]
    coarse_rows = fine_rows // 2
    lat_count = lax.axis_size("lat")
    lat_place = lax.axis_index("lat")
    fine_total = fine_rows * lat_count
    coarse_total = coarse_rows * lat_count
    fine_offset = lat_place * fine_rows
    coarse_offset = lat_place * coarse_rows
    grad_scale = (fine_total * tokens.shape[1] * lax.axis_size("lon") // 4) ** (-0.5)
    rolled_fine = rotate_ahead(tokens)
    fine_result, fine_saved = block_forward(
        rolled_fine, fine_gain, fine_qkv, fine_proj, fine_offset, fine_total, HF
    )
    fine_grid = rotate_ahead(fine_result)
    merged, merge_saved = merge_forward(fine_grid, merge_gain, merge_weight)
    rolled_coarse = merged
    coarse_result, coarse_saved = block_forward(
        rolled_coarse, coarse_gain, coarse_qkv, coarse_proj, coarse_offset, coarse_total, HC
    )
    output = rotate_back(coarse_result)
    grad_coarse_out = rotate_ahead(cotangent)
    grad_rolled_coarse, coarse_gain_sum, coarse_qkv_sum, coarse_proj_sum = block_backward(
        grad_coarse_out,
        rolled_coarse,
        coarse_gain,
        coarse_qkv,
        coarse_proj,
        coarse_saved,
        coarse_offset,
        coarse_total,
        HC,
    )
    grad_merged = grad_rolled_coarse
    grad_fine_grid, merge_gain_sum, merge_weight_sum = merge_backward(
        grad_merged, merge_saved, merge_gain, merge_weight
    )
    grad_fine_out = rotate_back(grad_fine_grid)
    grad_rolled_fine, fine_gain_sum, fine_qkv_sum, fine_proj_sum = block_backward(
        grad_fine_out,
        rolled_fine,
        fine_gain,
        fine_qkv,
        fine_proj,
        fine_saved,
        fine_offset,
        fine_total,
        HF,
    )
    grad_tokens = rotate_back(grad_rolled_fine)
    devices = lat_count * lax.axis_size("lon")

    def gather_sums(sums, width):
        pieces = [as_pieces(value, devices, width) for value in sums]
        total = reduce_pieces(jnp.concatenate(pieces, axis=1))
        found, start = [], 0
        for value, piece in zip(sums, pieces):
            part = total[start : start + piece.shape[1]]
            found.append(from_pieces(part, value.shape[0] // devices, value.shape[1]))
            start += piece.shape[1]
        return found

    merge_weight_sum, coarse_qkv_sum, coarse_proj_sum = gather_sums(
        (merge_weight_sum, coarse_qkv_sum, coarse_proj_sum), coarse_proj.shape[1]
    )
    fine_qkv_sum, fine_proj_sum = gather_sums((fine_qkv_sum, fine_proj_sum), 256)
    gains = [v.reshape(devices, -1) for v in (fine_gain_sum, merge_gain_sum, coarse_gain_sum)]
    gain_sums = reduce_pieces(jnp.concatenate(gains, axis=1)[:, None, :])[0]
    first, second = gains[0].shape[1], gains[0].shape[1] + gains[1].shape[1]
    fine_gain_sum, merge_gain_sum = gain_sums[:first], gain_sums[first:second]
    coarse_gain_sum = gain_sums[second:]
    return (
        output,
        grad_tokens,
        fine_gain_sum * grad_scale,
        fine_qkv_sum * grad_scale,
        fine_proj_sum * grad_scale,
        merge_gain_sum * grad_scale,
        merge_weight_sum * grad_scale,
        coarse_gain_sum * grad_scale,
        coarse_qkv_sum * grad_scale,
        coarse_proj_sum * grad_scale,
    )


def solution(mesh):
    return jax.shard_map(
        local,
        mesh=mesh,
        in_specs=(
            P("lat", "lon", None),
            P(),
            P(),
            P(),
            P(),
            P(),
            P(),
            P(),
            P(),
            P("lat", "lon", None),
        ),
        out_specs=(
            P("lat", "lon", None),
            P("lat", "lon", None),
            P(("lat", "lon")),
            P(("lat", "lon"), None),
            P(("lat", "lon"), None),
            P(("lat", "lon")),
            P(("lat", "lon"), None),
            P(("lat", "lon")),
            P(("lat", "lon"), None),
            P(("lat", "lon"), None),
        ),
        check_vma=False,
    )
```

```python
import functools

import jax
import jax.numpy as jnp
import numpy as np
from jax import lax
from jax.experimental import pallas as pl
from jax.experimental.pallas import tpu as pltpu
from jax.sharding import PartitionSpec as P

HF = 4
HC = 8
WLAT = 6
WLON = 12
SLAT = 3
SLON = 6


EPSILON = 1e-05


VMEM = pl.BlockSpec(memory_space=pltpu.VMEM)
SMEM = pl.BlockSpec(memory_space=pltpu.SMEM)
F32 = jnp.float32
BF16 = jnp.bfloat16


def one_hot(sources, size):
    matrix = np.zeros((len(sources), size), np.float32)
    for row, source in enumerate(sources):
        if source >= 0:
            matrix[row, source] = 1.0
    return jnp.asarray(matrix, BF16)


def window_order(rows, cols):
    return [
        (a * WLAT + i, b * WLON + j)
        for a in range(rows // WLAT)
        for b in range(cols // WLON)
        for i in range(WLAT)
        for j in range(WLON)
    ]


def merge_order(rows, cols):
    return [
        (2 * a + low, 2 * b + side)
        for side in range(2)
        for low in range(2)
        for a, b in window_order(rows // 2, cols // 2)
    ]


def natural_order(rows, cols):
    return [(i, j) for i in range(rows) for j in range(cols)]


def roll_parts(rows, cols, ahead):
    if ahead:
        lat, lon = (range(SLAT), range(SLAT, rows)), (range(SLON), range(SLON, cols))
    else:
        lat = (range(rows - SLAT, rows), range(rows - SLAT))
        lon = (range(cols - SLON, cols), range(cols - SLON))
    pick = ((lat[0], lon[1]), (lat[1], lon[0]), (lat[0], lon[0]))
    return [[(i, j) for i in r for j in c] for r, c in pick]


def roll_matrices(rows, cols, ahead, order):
    shift = 1 if ahead else -1
    parts = [{cell: k for k, cell in enumerate(p)} for p in roll_parts(rows, cols, ahead)]
    found = [[], [], [], []]
    for i, j in order:
        row, col = i + shift * SLAT, j + shift * SLON
        out_row, out_col = not 0 <= row < rows, not 0 <= col < cols
        cell = (row % rows, col % cols)
        which = {(0, 0): 0, (1, 0): 1, (0, 1): 2, (1, 1): 3}[(int(out_row), int(out_col))]
        for k in range(4):
            found[k].append((cell if k == 0 else parts[k - 1][cell]) if k == which else -1)
    return found, [len(p) for p in parts]


def assembling(rows, cols, ahead, order, stored):
    place = {cell: k for k, cell in enumerate(stored)}
    found, sizes = roll_matrices(rows, cols, ahead, order)
    own = [place[c] if c != -1 else -1 for c in found[0]]
    return [one_hot(own, rows * cols)] + [one_hot(f, n) for f, n in zip(found[1:], sizes)]


def sending(rows, cols, ahead, stored):
    place = {cell: k for k, cell in enumerate(stored)}
    return [
        one_hot([place[c] for c in part], rows * cols) for part in roll_parts(rows, cols, ahead)
    ]


def send_parts(parts, ahead):
    step = -1 if ahead else 1
    return [send(parts[0], step, 0), send(parts[1], 0, step), send(parts[2], step, step)]


def mm(left, right):
    return jnp.dot(left, right, preferred_element_type=F32)


def mm_t(left, right):
    return lax.dot_general(left, right, (((1,), (1,)), ((), ())), preferred_element_type=F32)


def t_mm(left, right):
    return lax.dot_general(left, right, (((0,), (0,)), ((), ())), preferred_element_type=F32)


def gathered(values, matrices):
    total = mm(matrices[0][...], values[0][...])
    for value, matrix in zip(values[1:], matrices[1:]):
        total = total + mm(matrix[...], value[...])
    return total


def norm_parts(values):
    center = jnp.mean(values, axis=-1, keepdims=True)
    shifted = values - center
    spread = jnp.mean(shifted * shifted, axis=-1, keepdims=True)
    rate = lax.rsqrt(spread + EPSILON)
    return shifted * rate, rate


def norm_back(grad, unit, rate, gains):
    scaled = grad * gains
    first = jnp.mean(scaled, axis=-1, keepdims=True)
    second = jnp.mean(scaled * unit, axis=-1, keepdims=True)
    return rate * (scaled - first - unit * second), jnp.sum(grad * unit, axis=0, keepdims=True)


def lane_halves(value, size):
    lane = lax.broadcasted_iota(jnp.int32, value.shape, 1)
    return [
        jnp.where((lane >= k * size) & (lane < (k + 1) * size), value, jnp.zeros_like(value))
        for k in range(value.shape[1] // size)
    ]


def stacked(value, size):
    return jnp.concatenate(lane_halves(value, size), axis=0).astype(BF16)


def unstacked(value, size):
    cells = value.shape[0] * size // value.shape[1]
    lane = lax.broadcasted_iota(jnp.int32, (cells, value.shape[1]), 1)
    total = value[:cells]
    for k in range(1, value.shape[1] // size):
        total = jnp.where(lane >= k * size, value[k * cells : (k + 1) * cells], total)
    return total


def weights_of(query, keys, border, size):
    cells = keys.shape[0]
    scores = mm_t(query, keys) * size ** (-0.5)
    row = lax.broadcasted_iota(jnp.int32, scores.shape, 0)
    other = lax.broadcasted_iota(jnp.int32, scores.shape, 1)
    for _ in range(query.shape[0] // cells - 1):
        row = jnp.where(row >= cells, row - cells, row)
    allowed = (row >= border).astype(jnp.int32) == (other >= border).astype(jnp.int32)
    scores = jnp.where(allowed, scores, -1000000000.0)
    exponent = jnp.exp(scores - jnp.max(scores, axis=-1, keepdims=True))
    return exponent * (1.0 / jnp.sum(exponent, axis=-1, keepdims=True)), allowed


def attention_groups(cells, heads, inner, windows_lon):
    size = inner // heads
    lanes = 128 if inner % 128 == 0 and 128 % size == 0 else inner
    count = WLAT * WLON
    for window in range(cells // count):
        for start in range(0, inner, lanes):
            rows = slice(window * count, (window + 1) * count)
            yield window // windows_lon, rows, start, lanes, size


def border_of(edge, window_row):
    return (edge - window_row * WLAT) * WLON


def attend(packed, mixed_ref, edge, heads, windows_lon):
    inner = packed.shape[1] // 3
    for w, rows, start, lanes, size in attention_groups(
        packed.shape[0], heads, inner, windows_lon
    ):
        query = stacked(packed[rows, start : start + lanes], size)
        keys = packed[rows, inner + start : inner + start + lanes].astype(BF16)
        vals = packed[rows, 2 * inner + start : 2 * inner + start + lanes].astype(BF16)
        weights, _ = weights_of(query, keys, border_of(edge, w), size)
        mixed_ref[rows, start : start + lanes] = unstacked(mm(weights.astype(BF16), vals), size)


def attend_back(packed, grad_mixed, grad_ref, edge, heads, windows_lon):
    inner = packed.shape[1] // 3
    for w, rows, start, lanes, size in attention_groups(
        packed.shape[0], heads, inner, windows_lon
    ):
        query = stacked(packed[rows, start : start + lanes], size)
        keys = packed[rows, inner + start : inner + start + lanes].astype(BF16)
        vals = packed[rows, 2 * inner + start : 2 * inner + start + lanes].astype(BF16)
        grad = stacked(grad_mixed[rows, start : start + lanes], size)
        weights, allowed = weights_of(query, keys, border_of(edge, w), size)
        grad_weights = mm_t(grad, vals).astype(BF16).astype(F32)
        grad_vals = t_mm(weights.astype(BF16), grad)
        along = jnp.sum(grad_weights * weights, axis=-1, keepdims=True)
        slope = jnp.where(allowed, weights * (grad_weights - along), 0.0) * size ** (-0.5)
        slope = slope.astype(BF16)
        grad_ref[rows, start : start + lanes] = unstacked(mm(slope, keys), size)
        grad_ref[rows, inner + start : inner + start + lanes] = t_mm(slope, query)
        grad_ref[rows, 2 * inner + start : 2 * inner + start + lanes] = grad_vals


def rounded(value):
    return value.astype(BF16).astype(F32)


def fine_forward_kernel(windows_lon, *refs):
    (edge, own, p0, p1, p2, m0, m1, m2, m3, s1, s2, s3, gains, w_qkv, w_proj) = refs[:15]
    (rolled_ref, packed_ref, mixed_ref, result_ref, o1, o2, o3, mixed) = refs[15:]
    rolled = gathered((own, p0, p1, p2), (m0, m1, m2, m3))
    rolled_ref[...] = rolled.astype(BF16)
    unit, _ = norm_parts(rolled)
    packed = rounded(mm((unit * gains[...]).astype(BF16), w_qkv[...]))
    packed_ref[...] = packed.astype(BF16)
    attend(packed, mixed, edge[0], HF, windows_lon)
    blend = mixed[...].astype(BF16)
    mixed_ref[...] = blend
    result = (rolled + mm(blend, w_proj[...])).astype(BF16)
    result_ref[...] = result
    for out, pick in ((o1, s1), (o2, s2), (o3, s3)):
        out[...] = mm(pick[...], result).astype(BF16)


def coarse_kernel(windows_lon, *refs):
    (edge, own, p0, p1, p2, m0, m1, m2, m3, own_c, c0, c1, c2, n0, n1, n2, n3) = refs[:17]
    (s1, s2, s3, merge_gain, w_merge, gains, w_qkv, w_proj) = refs[17:25]
    (result_ref, out_ref, o1, o2, o3, g_merge_gain, g_merge, g_gain, g_qkv, g_proj) = refs[25:35]
    mixed, grad_packed_ref = refs[35:]
    fine = gathered((own, p0, p1, p2), (m0, m1, m2, m3))
    cells = fine.shape[0] // 4
    grid = jnp.concatenate([fine[k * cells : (k + 1) * cells] for k in range(4)], axis=1)
    merge_unit, merge_rate = norm_parts(grid)
    merge_normed = (merge_unit * merge_gain[...]).astype(BF16)
    rolled = rounded(mm(merge_normed, w_merge[...]))
    unit, rate = norm_parts(rolled)
    normed = (unit * gains[...]).astype(BF16)
    packed = rounded(mm(normed, w_qkv[...]))
    attend(packed, mixed, edge[0], HC, windows_lon)
    blend = mixed[...].astype(BF16)
    result_ref[...] = (rolled + mm(blend, w_proj[...])).astype(BF16)
    grad_out = gathered((own_c, c0, c1, c2), (n0, n1, n2, n3))
    grad_out_low = grad_out.astype(BF16)
    g_proj[...] = t_mm(blend, grad_out_low).astype(BF16)
    grad_mixed = rounded(mm_t(grad_out_low, w_proj[...]))
    attend_back(packed, grad_mixed, grad_packed_ref, edge[0], HC, windows_lon)
    grad_packed = grad_packed_ref[...].astype(BF16)
    grad_normed = rounded(mm_t(grad_packed, w_qkv[...]))
    g_qkv[...] = t_mm(normed, grad_packed).astype(BF16)
    grad_in, gain_sum = norm_back(grad_normed, unit, rate, gains[...])
    g_gain[...] = gain_sum
    grad_rolled = (grad_out + grad_in).astype(BF16)
    grad_merge = rounded(mm_t(grad_rolled, w_merge[...]))
    g_merge[...] = t_mm(merge_normed, grad_rolled).astype(BF16)
    grad_grid, gain_sum = norm_back(grad_merge, merge_unit, merge_rate, merge_gain[...])
    g_merge_gain[...] = gain_sum
    breadth = fine.shape[1]
    parts = [grad_grid[:, k * breadth : (k + 1) * breadth] for k in range(4)]
    out = jnp.concatenate(parts, axis=0).astype(BF16)
    out_ref[...] = out
    for part, pick in ((o1, s1), (o2, s2), (o3, s3)):
        part[...] = mm(pick[...], out).astype(BF16)


def fine_backward_kernel(windows_lon, *refs):
    (edge, own, p0, p1, p2, m0, m1, m2, m3, s1, s2, s3) = refs[:12]
    (rolled_ref, packed_ref, mixed_ref, gains, w_qkv, w_proj) = refs[12:18]
    (out_ref, o1, o2, o3, g_gain, g_qkv, g_proj, grad_packed_ref) = refs[18:]
    grad_out = gathered((own, p0, p1, p2), (m0, m1, m2, m3))
    grad_out_low = grad_out.astype(BF16)
    g_proj[...] = t_mm(mixed_ref[...], grad_out_low).astype(BF16)
    grad_mixed = rounded(mm_t(grad_out_low, w_proj[...]))
    packed = packed_ref[...].astype(F32)
    attend_back(packed, grad_mixed, grad_packed_ref, edge[0], HF, windows_lon)
    grad_packed = grad_packed_ref[...].astype(BF16)
    grad_normed = rounded(mm_t(grad_packed, w_qkv[...]))
    unit, rate = norm_parts(rolled_ref[...].astype(F32))
    g_qkv[...] = t_mm((unit * gains[...]).astype(BF16), grad_packed).astype(BF16)
    grad_in, gain_sum = norm_back(grad_normed, unit, rate, gains[...])
    g_gain[...] = gain_sum
    grad_rolled = (grad_out + grad_in).astype(BF16)
    out_ref[...] = grad_rolled
    for part, pick in ((o1, s1), (o2, s2), (o3, s3)):
        part[...] = mm(pick[...], grad_rolled).astype(BF16)


def roll_kernel(own, p0, p1, p2, m0, m1, m2, m3, out):
    out[...] = gathered((own, p0, p1, p2), (m0, m1, m2, m3)).astype(BF16)


def call(body, name, operands, outs, scratch=(), scalar=False, flops=0):
    shapes = [jax.ShapeDtypeStruct(shape, dtype) for shape, dtype in outs]
    moved = sum(v.size * v.dtype.itemsize for v in operands)
    moved += sum(v.size * v.dtype.itemsize for v in shapes)
    return pl.pallas_call(
        body,
        name=name,
        out_shape=shapes,
        in_specs=[SMEM if scalar and k == 0 else VMEM for k in range(len(operands))],
        out_specs=[VMEM] * len(shapes),
        scratch_shapes=[pltpu.VMEM(shape, F32) for shape in scratch],
        compiler_params=pltpu.CompilerParams(vmem_limit_bytes=56 * 1024 * 1024),
        cost_estimate=pl.CostEstimate(flops=flops, bytes_accessed=moved, transcendentals=0),
    )(*operands)


def cut_parts(grid, ahead):
    if ahead:
        lat, lon = (slice(None, SLAT), slice(SLAT, None)), (slice(None, SLON), slice(SLON, None))
    else:
        lat = (slice(-SLAT, None), slice(None, -SLAT))
        lon = (slice(-SLON, None), slice(None, -SLON))
    picks = ((lat[0], lon[1]), (lat[1], lon[0]), (lat[0], lon[0]))
    return [grid[r, c].reshape(-1, grid.shape[2]) for r, c in picks]


def shift_pairs(lat_step, lon_step):
    lats, lons = lax.axis_size("lat"), lax.axis_size("lon")
    return [
        (a * lons + b, ((a + lat_step) % lats) * lons + (b + lon_step) % lons)
        for a in range(lats)
        for b in range(lons)
    ]


def send(value, lat_step, lon_step):
    return lax.ppermute(value, ("lat", "lon"), shift_pairs(lat_step, lon_step))


def rotate_back(grid):
    above = send(grid[-SLAT:, :-SLON], 1, 0)
    beside = send(grid[:-SLAT, -SLON:], 0, 1)
    corner = send(grid[-SLAT:, -SLON:], 1, 1)
    low = jnp.concatenate([beside, grid[:-SLAT, :-SLON]], axis=1)
    return jnp.concatenate([jnp.concatenate([corner, above], axis=1), low], axis=0)


def halve(value, axis, step):
    count = lax.axis_size(axis)
    bit = (lax.axis_index(axis) // step) % 2
    kept = lax.dynamic_index_in_dim(value, bit, 1, keepdims=False)
    gone = lax.dynamic_index_in_dim(value, 1 - bit, 1, keepdims=False)
    came = lax.ppermute(gone, axis, [(i, i ^ step) for i in range(count)])
    return (kept.astype(jnp.float32) + came.astype(jnp.float32)).astype(value.dtype)


def reduce_pieces(value):
    lats, lons = lax.axis_size("lat"), lax.axis_size("lon")
    rows, columns = value.shape[1:]
    if lats & (lats - 1) or lons & (lons - 1):
        total = lax.psum_scatter(value, ("lat", "lon"), scatter_dimension=0, tiled=True)
        return total.reshape(rows, columns)
    step = 1
    while step < lons:
        left = lons // step
        value = value.reshape(lats * left // 2, 2, rows, columns)
        value = halve(value, "lon", step)
        step *= 2
    step = 1
    while step < lats:
        left = lats // step
        value = value.reshape(left // 2, 2, rows, columns)
        value = halve(value, "lat", step)
        step *= 2
    return value.reshape(rows, columns)


def as_pieces(value, devices, width):
    rows = value.shape[0] // devices
    value = value.astype(jnp.bfloat16).reshape(devices, rows, value.shape[1])
    parts = [value[:, :, i : i + width] for i in range(0, value.shape[2], width)]
    return jnp.concatenate(parts, axis=1)


def from_pieces(value, rows, columns):
    width = value.shape[1]
    parts = [value[i * rows : (i + 1) * rows] for i in range(columns // width)]
    return jnp.concatenate(parts, axis=1).astype(jnp.float32)


def local(
    tokens,
    fine_gain,
    fine_qkv,
    fine_proj,
    merge_gain,
    merge_weight,
    coarse_gain,
    coarse_qkv,
    coarse_proj,
    cotangent,
):
    fine_rows = tokens.shape[0]
    coarse_rows = fine_rows // 2
    lat_count = lax.axis_size("lat")
    lat_place = lax.axis_index("lat")
    fine_total = fine_rows * lat_count
    coarse_total = coarse_rows * lat_count
    fine_offset = lat_place * fine_rows
    coarse_offset = lat_place * coarse_rows
    grad_scale = (fine_total * tokens.shape[1] * lax.axis_size("lon") // 4) ** (-0.5)
    fine_cols, coarse_cols = tokens.shape[1], tokens.shape[1] // 2
    cells, breadth = fine_rows * fine_cols, tokens.shape[2]
    coarse_cells, coarse_breadth = cells // 4, coarse_proj.shape[1]
    fine = (fine_rows, fine_cols)
    coarse = (coarse_rows, coarse_cols)
    fine_edge = jnp.reshape(fine_total - SLAT - fine_offset, (1,)).astype(jnp.int32)
    coarse_edge = jnp.reshape(coarse_total - SLAT - coarse_offset, (1,)).astype(jnp.int32)
    sizes = [len(part) for part in roll_parts(*fine, True)]
    part_outs = [((n, breadth), BF16) for n in sizes]
    windowed, natural, merged = window_order(*fine), natural_order(*fine), merge_order(*fine)

    arrived = send_parts(cut_parts(tokens, True), True)
    cotangent_parts = send_parts(cut_parts(cotangent, True), True)
    inner = fine_proj.shape[0]
    rolled_fine, packed, blend, result, *parts = call(
        functools.partial(fine_forward_kernel, fine_cols // WLON),
        "fine_forward",
        [fine_edge, tokens.reshape(cells, breadth)]
        + arrived
        + assembling(*fine, True, windowed, natural)
        + sending(*fine, True, windowed)
        + [fine_gain[None], fine_qkv, fine_proj],
        [((cells, breadth), BF16), ((cells, 3 * inner), BF16), ((cells, inner), BF16)]
        + [((cells, breadth), BF16)]
        + part_outs,
        [(cells, inner)],
        True,
        3 * 10**9,
    )
    arrived = send_parts(parts, True)
    coarse_inner = coarse_proj.shape[0]
    coarse_windowed = window_order(*coarse)
    found = call(
        functools.partial(coarse_kernel, coarse_cols // WLON),
        "coarse",
        [coarse_edge, result]
        + arrived
        + assembling(*fine, True, merged, windowed)
        + [cotangent.reshape(coarse_cells, coarse_breadth)]
        + cotangent_parts
        + assembling(*coarse, True, coarse_windowed, natural_order(*coarse))
        + sending(*fine, False, merged)
        + [merge_gain[None], merge_weight, coarse_gain[None], coarse_qkv, coarse_proj],
        [((coarse_cells, coarse_breadth), BF16), ((cells, breadth), BF16)]
        + part_outs
        + [((1, 4 * breadth), F32), (merge_weight.shape, BF16), ((1, coarse_breadth), F32)]
        + [(coarse_qkv.shape, BF16), (coarse_proj.shape, BF16)],
        [(coarse_cells, coarse_inner), (coarse_cells, 3 * coarse_inner)],
        True,
        9 * 10**9,
    )
    coarse_result, grad_grid = found[:2]
    merge_gain_sum, merge_weight_sum, coarse_gain_sum = found[5][0], found[6], found[7][0]
    coarse_qkv_sum, coarse_proj_sum = found[8:]
    arrived = send_parts(found[2:5], False)
    grad_rolled, *parts = call(
        functools.partial(fine_backward_kernel, fine_cols // WLON),
        "fine_backward",
        [fine_edge, grad_grid]
        + arrived
        + assembling(*fine, False, windowed, merged)
        + sending(*fine, False, windowed)
        + [rolled_fine, packed, blend, fine_gain[None], fine_qkv, fine_proj],
        [((cells, breadth), BF16)]
        + part_outs
        + [((1, breadth), F32), (fine_qkv.shape, BF16), (fine_proj.shape, BF16)],
        [(cells, 3 * inner)],
        True,
        6 * 10**9,
    )
    fine_gain_sum, fine_qkv_sum, fine_proj_sum = parts[3][0], parts[4], parts[5]
    arrived = send_parts(parts[:3], False)
    (grad_tokens,) = call(
        roll_kernel,
        "final_roll",
        [grad_rolled] + arrived + assembling(*fine, False, natural, windowed),
        [((cells, breadth), BF16)],
        flops=10**8,
    )
    grad_tokens = grad_tokens.reshape(tokens.shape)
    coarse_grid = coarse_result.reshape(coarse_rows // WLAT, coarse_cols // WLON, WLAT, WLON, -1)
    coarse_grid = coarse_grid.transpose(0, 2, 1, 3, 4).reshape(cotangent.shape)
    output = rotate_back(coarse_grid)
    devices = lat_count * lax.axis_size("lon")

    def gather_sums(sums, width):
        pieces = [as_pieces(value, devices, width) for value in sums]
        total = reduce_pieces(jnp.concatenate(pieces, axis=1))
        found, start = [], 0
        for value, piece in zip(sums, pieces):
            part = total[start : start + piece.shape[1]]
            found.append(from_pieces(part, value.shape[0] // devices, value.shape[1]))
            start += piece.shape[1]
        return found

    merge_weight_sum, coarse_qkv_sum, coarse_proj_sum = gather_sums(
        (merge_weight_sum, coarse_qkv_sum, coarse_proj_sum), coarse_proj.shape[1]
    )
    fine_qkv_sum, fine_proj_sum = gather_sums((fine_qkv_sum, fine_proj_sum), 256)
    gains = [v.reshape(devices, -1) for v in (fine_gain_sum, merge_gain_sum, coarse_gain_sum)]
    gain_sums = reduce_pieces(jnp.concatenate(gains, axis=1)[:, None, :])[0]
    first, second = gains[0].shape[1], gains[0].shape[1] + gains[1].shape[1]
    fine_gain_sum, merge_gain_sum = gain_sums[:first], gain_sums[first:second]
    coarse_gain_sum = gain_sums[second:]
    return (
        output,
        grad_tokens,
        fine_gain_sum * grad_scale,
        fine_qkv_sum * grad_scale,
        fine_proj_sum * grad_scale,
        merge_gain_sum * grad_scale,
        merge_weight_sum * grad_scale,
        coarse_gain_sum * grad_scale,
        coarse_qkv_sum * grad_scale,
        coarse_proj_sum * grad_scale,
    )


def solution(mesh):
    return jax.shard_map(
        local,
        mesh=mesh,
        in_specs=(
            P("lat", "lon", None),
            P(),
            P(),
            P(),
            P(),
            P(),
            P(),
            P(),
            P(),
            P("lat", "lon", None),
        ),
        out_specs=(
            P("lat", "lon", None),
            P("lat", "lon", None),
            P(("lat", "lon")),
            P(("lat", "lon"), None),
            P(("lat", "lon"), None),
            P(("lat", "lon")),
            P(("lat", "lon"), None),
            P(("lat", "lon")),
            P(("lat", "lon"), None),
            P(("lat", "lon"), None),
        ),
        check_vma=False,
    )
```

```python
import functools

import jax
import jax.numpy as jnp
import numpy as np
from jax import lax
from jax.experimental import pallas as pl
from jax.experimental.pallas import tpu as pltpu
from jax.sharding import PartitionSpec as P

HF = 4
HC = 8
WLAT = 6
WLON = 12
SLAT = 3
SLON = 6


EPSILON = 1e-05


VMEM = pl.BlockSpec(memory_space=pltpu.VMEM)
SMEM = pl.BlockSpec(memory_space=pltpu.SMEM)
F32 = jnp.float32
BF16 = jnp.bfloat16


def one_hot(sources, size):
    matrix = np.zeros((len(sources), size), np.float32)
    for row, source in enumerate(sources):
        if source >= 0:
            matrix[row, source] = 1.0
    return jnp.asarray(matrix, BF16)


def window_order(rows, cols):
    return [
        (a * WLAT + i, b * WLON + j)
        for a in range(rows // WLAT)
        for b in range(cols // WLON)
        for i in range(WLAT)
        for j in range(WLON)
    ]


def merge_order(rows, cols):
    return [
        (2 * a + low, 2 * b + side)
        for side in range(2)
        for low in range(2)
        for a, b in window_order(rows // 2, cols // 2)
    ]


def natural_order(rows, cols):
    return [(i, j) for i in range(rows) for j in range(cols)]


def roll_parts(rows, cols, ahead):
    if ahead:
        lat, lon = (range(SLAT), range(SLAT, rows)), (range(SLON), range(SLON, cols))
    else:
        lat = (range(rows - SLAT, rows), range(rows - SLAT))
        lon = (range(cols - SLON, cols), range(cols - SLON))
    pick = ((lat[0], lon[1]), (lat[1], lon[0]), (lat[0], lon[0]))
    return [[(i, j) for i in r for j in c] for r, c in pick]


def roll_matrices(rows, cols, ahead, order):
    shift = 1 if ahead else -1
    parts = [{cell: k for k, cell in enumerate(p)} for p in roll_parts(rows, cols, ahead)]
    found = [[], [], [], []]
    for i, j in order:
        row, col = i + shift * SLAT, j + shift * SLON
        out_row, out_col = not 0 <= row < rows, not 0 <= col < cols
        cell = (row % rows, col % cols)
        which = {(0, 0): 0, (1, 0): 1, (0, 1): 2, (1, 1): 3}[(int(out_row), int(out_col))]
        for k in range(4):
            found[k].append((cell if k == 0 else parts[k - 1][cell]) if k == which else -1)
    return found, [len(p) for p in parts]


def assembling(rows, cols, ahead, order, stored):
    place = {cell: k for k, cell in enumerate(stored)}
    found, sizes = roll_matrices(rows, cols, ahead, order)
    own = [place[c] if c != -1 else -1 for c in found[0]]
    return [one_hot(own, rows * cols)] + [one_hot(f, n) for f, n in zip(found[1:], sizes)]


def sending(rows, cols, ahead, stored):
    place = {cell: k for k, cell in enumerate(stored)}
    return [
        one_hot([place[c] for c in part], rows * cols) for part in roll_parts(rows, cols, ahead)
    ]


def send_parts(parts, ahead):
    step = -1 if ahead else 1
    return [send(parts[0], step, 0), send(parts[1], 0, step), send(parts[2], step, step)]


def mm(left, right):
    return jnp.dot(left, right, preferred_element_type=F32)


def mm_t(left, right):
    return lax.dot_general(left, right, (((1,), (1,)), ((), ())), preferred_element_type=F32)


def t_mm(left, right):
    return lax.dot_general(left, right, (((0,), (0,)), ((), ())), preferred_element_type=F32)


def gathered(values, matrices):
    total = mm(matrices[0][...], values[0][...])
    for value, matrix in zip(values[1:], matrices[1:]):
        total = total + mm(matrix[...], value[...])
    return total


def norm_parts(values):
    center = jnp.mean(values, axis=-1, keepdims=True)
    shifted = values - center
    spread = jnp.mean(shifted * shifted, axis=-1, keepdims=True)
    rate = lax.rsqrt(spread + EPSILON)
    return shifted * rate, rate


def norm_back(grad, unit, rate, gains):
    scaled = grad * gains
    first = jnp.mean(scaled, axis=-1, keepdims=True)
    second = jnp.mean(scaled * unit, axis=-1, keepdims=True)
    return rate * (scaled - first - unit * second), jnp.sum(grad * unit, axis=0, keepdims=True)


def lane_halves(value, size):
    lane = lax.broadcasted_iota(jnp.int32, value.shape, 1)
    return [
        jnp.where((lane >= k * size) & (lane < (k + 1) * size), value, jnp.zeros_like(value))
        for k in range(value.shape[1] // size)
    ]


def stacked(value, size):
    return jnp.concatenate(lane_halves(value, size), axis=0).astype(BF16)


def unstacked(value, size):
    cells = value.shape[0] * size // value.shape[1]
    lane = lax.broadcasted_iota(jnp.int32, (cells, value.shape[1]), 1)
    total = value[:cells]
    for k in range(1, value.shape[1] // size):
        total = jnp.where(lane >= k * size, value[k * cells : (k + 1) * cells], total)
    return total


def weights_of(query, keys, border, size):
    cells = keys.shape[0]
    scores = mm_t(query, keys) * size ** (-0.5)
    row = lax.broadcasted_iota(jnp.int32, scores.shape, 0)
    other = lax.broadcasted_iota(jnp.int32, scores.shape, 1)
    for _ in range(query.shape[0] // cells - 1):
        row = jnp.where(row >= cells, row - cells, row)
    allowed = (row >= border).astype(jnp.int32) == (other >= border).astype(jnp.int32)
    scores = jnp.where(allowed, scores, -1000000000.0)
    exponent = jnp.exp(scores - jnp.max(scores, axis=-1, keepdims=True))
    return exponent * (1.0 / jnp.sum(exponent, axis=-1, keepdims=True)), allowed


def attention_groups(cells, heads, inner, windows_lon):
    size = inner // heads
    lanes = 128 if inner % 128 == 0 and 128 % size == 0 else inner
    count = WLAT * WLON
    for window in range(cells // count):
        for start in range(0, inner, lanes):
            rows = slice(window * count, (window + 1) * count)
            yield window // windows_lon, rows, start, lanes, size


def border_of(edge, window_row):
    return (edge - window_row * WLAT) * WLON


def attend(packed, mixed_ref, edge, heads, windows_lon):
    inner = packed.shape[1] // 3
    for w, rows, start, lanes, size in attention_groups(
        packed.shape[0], heads, inner, windows_lon
    ):
        query = stacked(packed[rows, start : start + lanes], size)
        keys = packed[rows, inner + start : inner + start + lanes].astype(BF16)
        vals = packed[rows, 2 * inner + start : 2 * inner + start + lanes].astype(BF16)
        weights, _ = weights_of(query, keys, border_of(edge, w), size)
        mixed_ref[rows, start : start + lanes] = unstacked(mm(weights.astype(BF16), vals), size)


def attend_back(packed, grad_mixed, grad_ref, edge, heads, windows_lon):
    inner = packed.shape[1] // 3
    for w, rows, start, lanes, size in attention_groups(
        packed.shape[0], heads, inner, windows_lon
    ):
        query = stacked(packed[rows, start : start + lanes], size)
        keys = packed[rows, inner + start : inner + start + lanes].astype(BF16)
        vals = packed[rows, 2 * inner + start : 2 * inner + start + lanes].astype(BF16)
        grad = stacked(grad_mixed[rows, start : start + lanes], size)
        weights, allowed = weights_of(query, keys, border_of(edge, w), size)
        grad_weights = mm_t(grad, vals).astype(BF16).astype(F32)
        grad_vals = t_mm(weights.astype(BF16), grad)
        along = jnp.sum(grad_weights * weights, axis=-1, keepdims=True)
        slope = jnp.where(allowed, weights * (grad_weights - along), 0.0) * size ** (-0.5)
        slope = slope.astype(BF16)
        grad_ref[rows, start : start + lanes] = unstacked(mm(slope, keys), size)
        grad_ref[rows, inner + start : inner + start + lanes] = t_mm(slope, query)
        grad_ref[rows, 2 * inner + start : 2 * inner + start + lanes] = grad_vals


def rounded(value):
    return value.astype(BF16).astype(F32)


def fine_forward_kernel(windows_lon, *refs):
    (edge, own, p0, p1, p2, m0, m1, m2, m3, s1, s2, s3, gains, w_qkv, w_proj) = refs[:15]
    (rolled_ref, packed_ref, mixed_ref, result_ref, o1, o2, o3, mixed) = refs[15:]
    rolled = gathered((own, p0, p1, p2), (m0, m1, m2, m3))
    rolled_ref[...] = rolled.astype(BF16)
    unit, _ = norm_parts(rolled)
    packed = rounded(mm((unit * gains[...]).astype(BF16), w_qkv[...]))
    packed_ref[...] = packed.astype(BF16)
    attend(packed, mixed, edge[0], HF, windows_lon)
    blend = mixed[...].astype(BF16)
    mixed_ref[...] = blend
    result = (rolled + mm(blend, w_proj[...])).astype(BF16)
    result_ref[...] = result
    for out, pick in ((o1, s1), (o2, s2), (o3, s3)):
        out[...] = mm(pick[...], result).astype(BF16)


def coarse_kernel(windows_lon, *refs):
    (edge, own, p0, p1, p2, m0, m1, m2, m3, own_c, c0, c1, c2, n0, n1, n2, n3) = refs[:17]
    (s1, s2, s3, merge_gain, w_merge, gains, w_qkv, w_proj) = refs[17:25]
    (result_ref, out_ref, o1, o2, o3, g_merge_gain, g_merge, g_gain, g_qkv, g_proj) = refs[25:35]
    mixed, grad_packed_ref = refs[35:]
    fine = gathered((own, p0, p1, p2), (m0, m1, m2, m3))
    cells = fine.shape[0] // 4
    grid = jnp.concatenate([fine[k * cells : (k + 1) * cells] for k in range(4)], axis=1)
    merge_unit, merge_rate = norm_parts(grid)
    merge_normed = (merge_unit * merge_gain[...]).astype(BF16)
    rolled = rounded(mm(merge_normed, w_merge[...]))
    unit, rate = norm_parts(rolled)
    normed = (unit * gains[...]).astype(BF16)
    packed = rounded(mm(normed, w_qkv[...]))
    attend(packed, mixed, edge[0], HC, windows_lon)
    blend = mixed[...].astype(BF16)
    result_ref[...] = (rolled + mm(blend, w_proj[...])).astype(BF16)
    grad_out = gathered((own_c, c0, c1, c2), (n0, n1, n2, n3))
    grad_out_low = grad_out.astype(BF16)
    g_proj[...] = t_mm(blend, grad_out_low).astype(BF16)
    grad_mixed = rounded(mm_t(grad_out_low, w_proj[...]))
    attend_back(packed, grad_mixed, grad_packed_ref, edge[0], HC, windows_lon)
    grad_packed = grad_packed_ref[...].astype(BF16)
    grad_normed = rounded(mm_t(grad_packed, w_qkv[...]))
    g_qkv[...] = t_mm(normed, grad_packed).astype(BF16)
    grad_in, gain_sum = norm_back(grad_normed, unit, rate, gains[...])
    g_gain[...] = gain_sum
    grad_rolled = (grad_out + grad_in).astype(BF16)
    grad_merge = rounded(mm_t(grad_rolled, w_merge[...]))
    g_merge[...] = t_mm(merge_normed, grad_rolled).astype(BF16)
    grad_grid, gain_sum = norm_back(grad_merge, merge_unit, merge_rate, merge_gain[...])
    g_merge_gain[...] = gain_sum
    breadth = fine.shape[1]
    parts = [grad_grid[:, k * breadth : (k + 1) * breadth] for k in range(4)]
    out = jnp.concatenate(parts, axis=0).astype(BF16)
    out_ref[...] = out
    for part, pick in ((o1, s1), (o2, s2), (o3, s3)):
        part[...] = mm(pick[...], out).astype(BF16)


def fine_backward_kernel(windows_lon, *refs):
    (edge, own, p0, p1, p2, m0, m1, m2, m3, s1, s2, s3) = refs[:12]
    (rolled_ref, packed_ref, mixed_ref, gains, w_qkv, w_proj) = refs[12:18]
    (out_ref, o1, o2, o3, g_gain, g_qkv, g_proj, grad_packed_ref) = refs[18:]
    grad_out = gathered((own, p0, p1, p2), (m0, m1, m2, m3))
    grad_out_low = grad_out.astype(BF16)
    g_proj[...] = t_mm(mixed_ref[...], grad_out_low).astype(BF16)
    grad_mixed = rounded(mm_t(grad_out_low, w_proj[...]))
    packed = packed_ref[...].astype(F32)
    attend_back(packed, grad_mixed, grad_packed_ref, edge[0], HF, windows_lon)
    grad_packed = grad_packed_ref[...].astype(BF16)
    grad_normed = rounded(mm_t(grad_packed, w_qkv[...]))
    unit, rate = norm_parts(rolled_ref[...].astype(F32))
    g_qkv[...] = t_mm((unit * gains[...]).astype(BF16), grad_packed).astype(BF16)
    grad_in, gain_sum = norm_back(grad_normed, unit, rate, gains[...])
    g_gain[...] = gain_sum
    grad_rolled = (grad_out + grad_in).astype(BF16)
    out_ref[...] = grad_rolled
    for part, pick in ((o1, s1), (o2, s2), (o3, s3)):
        part[...] = mm(pick[...], grad_rolled).astype(BF16)


def roll_kernel(own, p0, p1, p2, m0, m1, m2, m3, out):
    out[...] = gathered((own, p0, p1, p2), (m0, m1, m2, m3)).astype(BF16)


def call(body, name, operands, outs, scratch=(), scalar=False, flops=0):
    shapes = [jax.ShapeDtypeStruct(shape, dtype) for shape, dtype in outs]
    moved = sum(v.size * v.dtype.itemsize for v in operands)
    moved += sum(v.size * v.dtype.itemsize for v in shapes)
    return pl.pallas_call(
        body,
        name=name,
        out_shape=shapes,
        in_specs=[SMEM if scalar and k == 0 else VMEM for k in range(len(operands))],
        out_specs=[VMEM] * len(shapes),
        scratch_shapes=[pltpu.VMEM(shape, F32) for shape in scratch],
        compiler_params=pltpu.CompilerParams(vmem_limit_bytes=56 * 1024 * 1024),
        cost_estimate=pl.CostEstimate(flops=flops, bytes_accessed=moved, transcendentals=0),
    )(*operands)


def cut_parts(grid, ahead):
    if ahead:
        lat, lon = (slice(None, SLAT), slice(SLAT, None)), (slice(None, SLON), slice(SLON, None))
    else:
        lat = (slice(-SLAT, None), slice(None, -SLAT))
        lon = (slice(-SLON, None), slice(None, -SLON))
    picks = ((lat[0], lon[1]), (lat[1], lon[0]), (lat[0], lon[0]))
    return [grid[r, c].reshape(-1, grid.shape[2]) for r, c in picks]


def shift_pairs(lat_step, lon_step):
    lats, lons = lax.axis_size("lat"), lax.axis_size("lon")
    return [
        (a * lons + b, ((a + lat_step) % lats) * lons + (b + lon_step) % lons)
        for a in range(lats)
        for b in range(lons)
    ]


def send(value, lat_step, lon_step):
    return lax.ppermute(value, ("lat", "lon"), shift_pairs(lat_step, lon_step))


def rotate_back(grid):
    above = send(grid[-SLAT:, :-SLON], 1, 0)
    beside = send(grid[:-SLAT, -SLON:], 0, 1)
    corner = send(grid[-SLAT:, -SLON:], 1, 1)
    low = jnp.concatenate([beside, grid[:-SLAT, :-SLON]], axis=1)
    return jnp.concatenate([jnp.concatenate([corner, above], axis=1), low], axis=0)


def hop_orders():
    lons = [("lon", 1 << k) for k in range(lax.axis_size("lon").bit_length() - 1)]
    lats = [("lat", 1 << k) for k in range(lax.axis_size("lat").bit_length() - 1)]
    first, rest = lons[:1], lons[1:]
    return (
        first + rest + lats,
        first + rest[::-1] + lats,
        first + lats[:1] + rest + lats[1:],
    )


def sum_kernel(orders, *refs):
    count = len(orders)
    hops = len(orders[0])
    sources, outs = refs[:count], refs[count : 2 * count]
    lands = [refs[2 * count + c * hops : 2 * count + (c + 1) * hops] for c in range(count)]
    send_sem, recv_sem = refs[2 * count + count * hops :]
    place = {"lat": lax.axis_index("lat"), "lon": lax.axis_index("lon")}

    def bit_of(axis, step):
        return (place[axis] // step) % 2

    def partner(axis, step):
        where = dict(place)
        where[axis] = place[axis] + step - 2 * step * bit_of(axis, step)
        return (where["lat"], where["lon"])

    barrier = pltpu.get_barrier_semaphore()
    for axis, step in orders[0]:
        pl.semaphore_signal(
            barrier, inc=1, device_id=partner(axis, step), device_id_type=pl.DeviceIdType.MESH
        )
    pl.semaphore_wait(barrier, hops)

    def begin(chunk, hop):
        axis, step = orders[chunk][hop]
        source = sources[chunk] if hop == 0 else lands[chunk][hop - 1]
        half = source.shape[0] // 2
        copy = pltpu.make_async_remote_copy(
            src_ref=source.at[pl.ds((1 - bit_of(axis, step)) * half, half)],
            dst_ref=lands[chunk][hop],
            send_sem=send_sem.at[chunk, hop],
            recv_sem=recv_sem.at[chunk, hop],
            device_id=partner(axis, step),
            device_id_type=pl.DeviceIdType.MESH,
        )
        copy.start()
        return copy

    flying = [begin(chunk, 0) for chunk in range(count)]
    for hop in range(hops):
        for chunk in range(count):
            axis, step = orders[chunk][hop]
            flying[chunk].wait()
            source = sources[chunk] if hop == 0 else lands[chunk][hop - 1]
            land = lands[chunk][hop]
            half = land.shape[0]
            start = bit_of(axis, step) * half
            target = land if hop < hops - 1 else outs[chunk]

            def add(piece, carry):
                total = land[piece].astype(F32) + source[start + piece].astype(F32)
                target[piece] = total.astype(target.dtype)
                return carry

            lax.fori_loop(0, half, add, 0)
            if hop < hops - 1:
                flying[chunk] = begin(chunk, hop + 1)


def reduce_chunks(chunks):
    lats, lons = lax.axis_size("lat"), lax.axis_size("lon")
    if lats & (lats - 1) or lons & (lons - 1) or lats < 2 or lons < 2:
        return [
            lax.psum_scatter(c, ("lat", "lon"), scatter_dimension=0, tiled=True)[0].astype(F32)
            for c in chunks
        ]
    orders = hop_orders()[: len(chunks)]
    hops = len(orders[0])
    highest = [("lat", 1 << k) for k in reversed(range(lats.bit_length() - 1))]
    highest += [("lon", 1 << k) for k in reversed(range(lons.bit_length() - 1))]
    ready, lands, outs = [], [], []
    for chunk, order in zip(chunks, orders):
        tail = chunk.shape[1:]
        moved = chunk.reshape([2] * hops + list(tail))
        axes = [highest.index(bit) for bit in order] + [hops, hops + 1]
        ready.append(moved.transpose(axes).reshape(chunk.shape))
        lands += [pltpu.VMEM((1 << (hops - 1 - k),) + tail, BF16) for k in range(hops)]
        outs.append(jax.ShapeDtypeStruct((1,) + tail, F32))
    sums = pl.pallas_call(
        functools.partial(sum_kernel, orders),
        name="gradient_sums",
        out_shape=outs,
        in_specs=[VMEM] * len(ready),
        out_specs=[VMEM] * len(ready),
        scratch_shapes=lands
        + [pltpu.SemaphoreType.DMA((len(ready), hops)), pltpu.SemaphoreType.DMA((len(ready), hops))],
        compiler_params=pltpu.CompilerParams(
            collective_id=0, has_side_effects=True, vmem_limit_bytes=40 * 1024 * 1024
        ),
        cost_estimate=pl.CostEstimate(flops=10**7, bytes_accessed=10**8, transcendentals=0),
    )(*ready)
    return [value[0] for value in sums]


def as_pieces(value, devices, width):
    rows = value.shape[0] // devices
    value = value.astype(jnp.bfloat16).reshape(devices, rows, value.shape[1])
    parts = [value[:, :, i : i + width] for i in range(0, value.shape[2], width)]
    return jnp.concatenate(parts, axis=1)


def from_pieces(value, rows, columns):
    width = value.shape[1]
    parts = [value[i * rows : (i + 1) * rows] for i in range(columns // width)]
    return jnp.concatenate(parts, axis=1).astype(jnp.float32)


def local(
    tokens,
    fine_gain,
    fine_qkv,
    fine_proj,
    merge_gain,
    merge_weight,
    coarse_gain,
    coarse_qkv,
    coarse_proj,
    cotangent,
):
    fine_rows = tokens.shape[0]
    coarse_rows = fine_rows // 2
    lat_count = lax.axis_size("lat")
    lat_place = lax.axis_index("lat")
    fine_total = fine_rows * lat_count
    coarse_total = coarse_rows * lat_count
    fine_offset = lat_place * fine_rows
    coarse_offset = lat_place * coarse_rows
    grad_scale = (fine_total * tokens.shape[1] * lax.axis_size("lon") // 4) ** (-0.5)
    fine_cols, coarse_cols = tokens.shape[1], tokens.shape[1] // 2
    cells, breadth = fine_rows * fine_cols, tokens.shape[2]
    coarse_cells, coarse_breadth = cells // 4, coarse_proj.shape[1]
    fine = (fine_rows, fine_cols)
    coarse = (coarse_rows, coarse_cols)
    fine_edge = jnp.reshape(fine_total - SLAT - fine_offset, (1,)).astype(jnp.int32)
    coarse_edge = jnp.reshape(coarse_total - SLAT - coarse_offset, (1,)).astype(jnp.int32)
    sizes = [len(part) for part in roll_parts(*fine, True)]
    part_outs = [((n, breadth), BF16) for n in sizes]
    windowed, natural, merged = window_order(*fine), natural_order(*fine), merge_order(*fine)

    arrived = send_parts(cut_parts(tokens, True), True)
    cotangent_parts = send_parts(cut_parts(cotangent, True), True)
    inner = fine_proj.shape[0]
    rolled_fine, packed, blend, result, *parts = call(
        functools.partial(fine_forward_kernel, fine_cols // WLON),
        "fine_forward",
        [fine_edge, tokens.reshape(cells, breadth)]
        + arrived
        + assembling(*fine, True, windowed, natural)
        + sending(*fine, True, windowed)
        + [fine_gain[None], fine_qkv, fine_proj],
        [((cells, breadth), BF16), ((cells, 3 * inner), BF16), ((cells, inner), BF16)]
        + [((cells, breadth), BF16)]
        + part_outs,
        [(cells, inner)],
        True,
        3 * 10**9,
    )
    arrived = send_parts(parts, True)
    coarse_inner = coarse_proj.shape[0]
    coarse_windowed = window_order(*coarse)
    found = call(
        functools.partial(coarse_kernel, coarse_cols // WLON),
        "coarse",
        [coarse_edge, result]
        + arrived
        + assembling(*fine, True, merged, windowed)
        + [cotangent.reshape(coarse_cells, coarse_breadth)]
        + cotangent_parts
        + assembling(*coarse, True, coarse_windowed, natural_order(*coarse))
        + sending(*fine, False, merged)
        + [merge_gain[None], merge_weight, coarse_gain[None], coarse_qkv, coarse_proj],
        [((coarse_cells, coarse_breadth), BF16), ((cells, breadth), BF16)]
        + part_outs
        + [((1, 4 * breadth), F32), (merge_weight.shape, BF16), ((1, coarse_breadth), F32)]
        + [(coarse_qkv.shape, BF16), (coarse_proj.shape, BF16)],
        [(coarse_cells, coarse_inner), (coarse_cells, 3 * coarse_inner)],
        True,
        9 * 10**9,
    )
    coarse_result, grad_grid = found[:2]
    merge_gain_sum, merge_weight_sum, coarse_gain_sum = found[5][0], found[6], found[7][0]
    coarse_qkv_sum, coarse_proj_sum = found[8:]
    arrived = send_parts(found[2:5], False)
    grad_rolled, *parts = call(
        functools.partial(fine_backward_kernel, fine_cols // WLON),
        "fine_backward",
        [fine_edge, grad_grid]
        + arrived
        + assembling(*fine, False, windowed, merged)
        + sending(*fine, False, windowed)
        + [rolled_fine, packed, blend, fine_gain[None], fine_qkv, fine_proj],
        [((cells, breadth), BF16)]
        + part_outs
        + [((1, breadth), F32), (fine_qkv.shape, BF16), (fine_proj.shape, BF16)],
        [(cells, 3 * inner)],
        True,
        6 * 10**9,
    )
    fine_gain_sum, fine_qkv_sum, fine_proj_sum = parts[3][0], parts[4], parts[5]
    arrived = send_parts(parts[:3], False)
    (grad_tokens,) = call(
        roll_kernel,
        "final_roll",
        [grad_rolled] + arrived + assembling(*fine, False, natural, windowed),
        [((cells, breadth), BF16)],
        flops=10**8,
    )
    grad_tokens = grad_tokens.reshape(tokens.shape)
    coarse_grid = coarse_result.reshape(coarse_rows // WLAT, coarse_cols // WLON, WLAT, WLON, -1)
    coarse_grid = coarse_grid.transpose(0, 2, 1, 3, 4).reshape(cotangent.shape)
    output = rotate_back(coarse_grid)
    devices = lat_count * lax.axis_size("lon")

    gains = [v.reshape(devices, 1, -1) for v in (fine_gain_sum, merge_gain_sum, coarse_gain_sum)]
    gain_rows = jnp.concatenate(gains, axis=2).astype(BF16)
    gain_rows = jnp.pad(gain_rows, ((0, 0), (0, 15), (0, 256 - gain_rows.shape[2])))
    width = merge_weight.shape[1]
    mixed = [as_pieces(v, devices, 256) for v in (coarse_proj_sum, fine_qkv_sum, fine_proj_sum)]
    heights = [v.shape[1] for v in mixed]
    merge_weight_total, coarse_qkv_total, total = reduce_chunks(
        [
            as_pieces(merge_weight_sum, devices, width),
            as_pieces(coarse_qkv_sum, devices, width),
            jnp.concatenate(mixed + [gain_rows], axis=1),
        ]
    )
    merge_weight_sum = merge_weight_total
    coarse_qkv_sum = from_pieces(
        coarse_qkv_total, coarse_qkv.shape[0] // devices, coarse_qkv.shape[1]
    )
    starts = [0, heights[0], heights[0] + heights[1], sum(heights)]
    coarse_proj_sum, fine_qkv_sum, fine_proj_sum = [
        from_pieces(total[starts[k] : starts[k + 1]], w.shape[0] // devices, w.shape[1])
        for k, w in enumerate((coarse_proj, fine_qkv, fine_proj))
    ]
    first, second = gains[0].shape[2], gains[0].shape[2] + gains[1].shape[2]
    gain_sums = total[starts[3]]
    fine_gain_sum, merge_gain_sum = gain_sums[:first], gain_sums[first:second]
    coarse_gain_sum = gain_sums[second : second + gains[2].shape[2]]
    return (
        output,
        grad_tokens,
        fine_gain_sum * grad_scale,
        fine_qkv_sum * grad_scale,
        fine_proj_sum * grad_scale,
        merge_gain_sum * grad_scale,
        merge_weight_sum * grad_scale,
        coarse_gain_sum * grad_scale,
        coarse_qkv_sum * grad_scale,
        coarse_proj_sum * grad_scale,
    )


def solution(mesh):
    return jax.shard_map(
        local,
        mesh=mesh,
        in_specs=(
            P("lat", "lon", None),
            P(),
            P(),
            P(),
            P(),
            P(),
            P(),
            P(),
            P(),
            P("lat", "lon", None),
        ),
        out_specs=(
            P("lat", "lon", None),
            P("lat", "lon", None),
            P(("lat", "lon")),
            P(("lat", "lon"), None),
            P(("lat", "lon"), None),
            P(("lat", "lon")),
            P(("lat", "lon"), None),
            P(("lat", "lon")),
            P(("lat", "lon"), None),
            P(("lat", "lon"), None),
        ),
        check_vma=False,
    )
```

```python
import functools

import jax
import jax.numpy as jnp
import numpy as np
from jax import lax
from jax.experimental import pallas as pl
from jax.experimental.pallas import tpu as pltpu
from jax.sharding import PartitionSpec as P

HF = 4
HC = 8
WLAT = 6
WLON = 12
SLAT = 3
SLON = 6


EPSILON = 1e-05


VMEM = pl.BlockSpec(memory_space=pltpu.VMEM)
SMEM = pl.BlockSpec(memory_space=pltpu.SMEM)
F32 = jnp.float32
BF16 = jnp.bfloat16


def one_hot(sources, size):
    matrix = np.zeros((len(sources), size), np.float32)
    for row, source in enumerate(sources):
        if source >= 0:
            matrix[row, source] = 1.0
    return jnp.asarray(matrix, BF16)


def window_order(rows, cols):
    return [
        (a * WLAT + i, b * WLON + j)
        for a in range(rows // WLAT)
        for b in range(cols // WLON)
        for i in range(WLAT)
        for j in range(WLON)
    ]


def merge_order(rows, cols):
    return [
        (2 * a + low, 2 * b + side)
        for side in range(2)
        for low in range(2)
        for a, b in window_order(rows // 2, cols // 2)
    ]


def natural_order(rows, cols):
    return [(i, j) for i in range(rows) for j in range(cols)]


def roll_parts(rows, cols, ahead):
    if ahead:
        lat, lon = (range(SLAT), range(SLAT, rows)), (range(SLON), range(SLON, cols))
    else:
        lat = (range(rows - SLAT, rows), range(rows - SLAT))
        lon = (range(cols - SLON, cols), range(cols - SLON))
    pick = ((lat[0], lon[1]), (lat[1], lon[0]), (lat[0], lon[0]))
    return [[(i, j) for i in r for j in c] for r, c in pick]


def roll_matrices(rows, cols, ahead, order):
    shift = 1 if ahead else -1
    parts = [{cell: k for k, cell in enumerate(p)} for p in roll_parts(rows, cols, ahead)]
    found = [[], [], [], []]
    for i, j in order:
        row, col = i + shift * SLAT, j + shift * SLON
        out_row, out_col = not 0 <= row < rows, not 0 <= col < cols
        cell = (row % rows, col % cols)
        which = {(0, 0): 0, (1, 0): 1, (0, 1): 2, (1, 1): 3}[(int(out_row), int(out_col))]
        for k in range(4):
            found[k].append((cell if k == 0 else parts[k - 1][cell]) if k == which else -1)
    return found, [len(p) for p in parts]


def assembling(rows, cols, ahead, order, stored):
    place = {cell: k for k, cell in enumerate(stored)}
    found, sizes = roll_matrices(rows, cols, ahead, order)
    own = [place[c] if c != -1 else -1 for c in found[0]]
    return [one_hot(own, rows * cols)] + [one_hot(f, n) for f, n in zip(found[1:], sizes)]


def sending(rows, cols, ahead, stored):
    place = {cell: k for k, cell in enumerate(stored)}
    return [
        one_hot([place[c] for c in part], rows * cols) for part in roll_parts(rows, cols, ahead)
    ]


def send_parts(parts, ahead):
    step = -1 if ahead else 1
    return [send(parts[0], step, 0), send(parts[1], 0, step), send(parts[2], step, step)]


def mm(left, right):
    return jnp.dot(left, right, preferred_element_type=F32)


def mm_t(left, right):
    return lax.dot_general(left, right, (((1,), (1,)), ((), ())), preferred_element_type=F32)


def t_mm(left, right):
    return lax.dot_general(left, right, (((0,), (0,)), ((), ())), preferred_element_type=F32)


def gathered(values, matrices):
    total = mm(matrices[0][...], values[0][...])
    for value, matrix in zip(values[1:], matrices[1:]):
        total = total + mm(matrix[...], value[...])
    return total


def norm_parts(values):
    center = jnp.mean(values, axis=-1, keepdims=True)
    shifted = values - center
    spread = jnp.mean(shifted * shifted, axis=-1, keepdims=True)
    rate = lax.rsqrt(spread + EPSILON)
    return shifted * rate, rate


def norm_back(grad, unit, rate, gains):
    scaled = grad * gains
    first = jnp.mean(scaled, axis=-1, keepdims=True)
    second = jnp.mean(scaled * unit, axis=-1, keepdims=True)
    return rate * (scaled - first - unit * second), jnp.sum(grad * unit, axis=0, keepdims=True)


def lane_halves(value, size):
    lane = lax.broadcasted_iota(jnp.int32, value.shape, 1)
    return [
        jnp.where((lane >= k * size) & (lane < (k + 1) * size), value, jnp.zeros_like(value))
        for k in range(value.shape[1] // size)
    ]


def stacked(value, size):
    return jnp.concatenate(lane_halves(value, size), axis=0).astype(BF16)


def unstacked(value, size):
    cells = value.shape[0] * size // value.shape[1]
    lane = lax.broadcasted_iota(jnp.int32, (cells, value.shape[1]), 1)
    total = value[:cells]
    for k in range(1, value.shape[1] // size):
        total = jnp.where(lane >= k * size, value[k * cells : (k + 1) * cells], total)
    return total


def weights_of(query, keys, border, size):
    cells = keys.shape[0]
    scores = mm_t(query, keys) * size ** (-0.5)
    row = lax.broadcasted_iota(jnp.int32, scores.shape, 0)
    other = lax.broadcasted_iota(jnp.int32, scores.shape, 1)
    for _ in range(query.shape[0] // cells - 1):
        row = jnp.where(row >= cells, row - cells, row)
    allowed = (row >= border).astype(jnp.int32) == (other >= border).astype(jnp.int32)
    scores = jnp.where(allowed, scores, -1000000000.0)
    exponent = jnp.exp(scores - jnp.max(scores, axis=-1, keepdims=True))
    return exponent * (1.0 / jnp.sum(exponent, axis=-1, keepdims=True)), allowed


def attention_groups(cells, heads, inner, windows_lon):
    size = inner // heads
    lanes = 128 if inner % 128 == 0 and 128 % size == 0 else inner
    count = WLAT * WLON
    for window in range(cells // count):
        for start in range(0, inner, lanes):
            rows = slice(window * count, (window + 1) * count)
            yield window // windows_lon, rows, start, lanes, size


def border_of(edge, window_row):
    return (edge - window_row * WLAT) * WLON


def attend(packed, mixed_ref, edge, heads, windows_lon):
    inner = packed.shape[1] // 3
    for w, rows, start, lanes, size in attention_groups(
        packed.shape[0], heads, inner, windows_lon
    ):
        query = stacked(packed[rows, start : start + lanes], size)
        keys = packed[rows, inner + start : inner + start + lanes].astype(BF16)
        vals = packed[rows, 2 * inner + start : 2 * inner + start + lanes].astype(BF16)
        weights, _ = weights_of(query, keys, border_of(edge, w), size)
        mixed_ref[rows, start : start + lanes] = unstacked(mm(weights.astype(BF16), vals), size)


def attend_back(packed, grad_mixed, grad_ref, edge, heads, windows_lon):
    inner = packed.shape[1] // 3
    for w, rows, start, lanes, size in attention_groups(
        packed.shape[0], heads, inner, windows_lon
    ):
        query = stacked(packed[rows, start : start + lanes], size)
        keys = packed[rows, inner + start : inner + start + lanes].astype(BF16)
        vals = packed[rows, 2 * inner + start : 2 * inner + start + lanes].astype(BF16)
        grad = stacked(grad_mixed[rows, start : start + lanes], size)
        weights, allowed = weights_of(query, keys, border_of(edge, w), size)
        grad_weights = mm_t(grad, vals).astype(BF16).astype(F32)
        grad_vals = t_mm(weights.astype(BF16), grad)
        along = jnp.sum(grad_weights * weights, axis=-1, keepdims=True)
        slope = jnp.where(allowed, weights * (grad_weights - along), 0.0) * size ** (-0.5)
        slope = slope.astype(BF16)
        grad_ref[rows, start : start + lanes] = unstacked(mm(slope, keys), size)
        grad_ref[rows, inner + start : inner + start + lanes] = t_mm(slope, query)
        grad_ref[rows, 2 * inner + start : 2 * inner + start + lanes] = grad_vals


def rounded(value):
    return value.astype(BF16).astype(F32)


def fine_forward_kernel(windows_lon, *refs):
    (edge, own, p0, p1, p2, m0, m1, m2, m3, s1, s2, s3, gains, w_qkv, w_proj) = refs[:15]
    (rolled_ref, packed_ref, mixed_ref, result_ref, o1, o2, o3, mixed) = refs[15:]
    rolled = gathered((own, p0, p1, p2), (m0, m1, m2, m3))
    rolled_ref[...] = rolled.astype(BF16)
    unit, _ = norm_parts(rolled)
    packed = rounded(mm((unit * gains[...]).astype(BF16), w_qkv[...]))
    packed_ref[...] = packed.astype(BF16)
    attend(packed, mixed, edge[0], HF, windows_lon)
    blend = mixed[...].astype(BF16)
    mixed_ref[...] = blend
    result = (rolled + mm(blend, w_proj[...])).astype(BF16)
    result_ref[...] = result
    for out, pick in ((o1, s1), (o2, s2), (o3, s3)):
        out[...] = mm(pick[...], result).astype(BF16)


def coarse_kernel(windows_lon, *refs):
    (edge, own, p0, p1, p2, m0, m1, m2, m3, own_c, c0, c1, c2, n0, n1, n2, n3) = refs[:17]
    (s1, s2, s3, merge_gain, w_merge, gains, w_qkv, w_proj) = refs[17:25]
    (result_ref, out_ref, o1, o2, o3, g_merge_gain, g_merge, g_gain, g_qkv, g_proj) = refs[25:35]
    mixed, grad_packed_ref = refs[35:]
    fine = gathered((own, p0, p1, p2), (m0, m1, m2, m3))
    cells = fine.shape[0] // 4
    grid = jnp.concatenate([fine[k * cells : (k + 1) * cells] for k in range(4)], axis=1)
    merge_unit, merge_rate = norm_parts(grid)
    merge_normed = (merge_unit * merge_gain[...]).astype(BF16)
    rolled = rounded(mm(merge_normed, w_merge[...]))
    unit, rate = norm_parts(rolled)
    normed = (unit * gains[...]).astype(BF16)
    packed = rounded(mm(normed, w_qkv[...]))
    attend(packed, mixed, edge[0], HC, windows_lon)
    blend = mixed[...].astype(BF16)
    result_ref[...] = (rolled + mm(blend, w_proj[...])).astype(BF16)
    grad_out = gathered((own_c, c0, c1, c2), (n0, n1, n2, n3))
    grad_out_low = grad_out.astype(BF16)
    g_proj[...] = t_mm(blend, grad_out_low).astype(BF16)
    grad_mixed = rounded(mm_t(grad_out_low, w_proj[...]))
    attend_back(packed, grad_mixed, grad_packed_ref, edge[0], HC, windows_lon)
    grad_packed = grad_packed_ref[...].astype(BF16)
    grad_normed = rounded(mm_t(grad_packed, w_qkv[...]))
    g_qkv[...] = t_mm(normed, grad_packed).astype(BF16)
    grad_in, gain_sum = norm_back(grad_normed, unit, rate, gains[...])
    g_gain[...] = gain_sum
    grad_rolled = (grad_out + grad_in).astype(BF16)
    grad_merge = rounded(mm_t(grad_rolled, w_merge[...]))
    g_merge[...] = t_mm(merge_normed, grad_rolled).astype(BF16)
    grad_grid, gain_sum = norm_back(grad_merge, merge_unit, merge_rate, merge_gain[...])
    g_merge_gain[...] = gain_sum
    breadth = fine.shape[1]
    parts = [grad_grid[:, k * breadth : (k + 1) * breadth] for k in range(4)]
    out = jnp.concatenate(parts, axis=0).astype(BF16)
    out_ref[...] = out
    for part, pick in ((o1, s1), (o2, s2), (o3, s3)):
        part[...] = mm(pick[...], out).astype(BF16)


def fine_backward_kernel(windows_lon, *refs):
    (edge, own, p0, p1, p2, m0, m1, m2, m3, s1, s2, s3) = refs[:12]
    (rolled_ref, packed_ref, mixed_ref, gains, w_qkv, w_proj) = refs[12:18]
    (out_ref, o1, o2, o3, g_gain, g_qkv, g_proj, grad_packed_ref) = refs[18:]
    grad_out = gathered((own, p0, p1, p2), (m0, m1, m2, m3))
    grad_out_low = grad_out.astype(BF16)
    g_proj[...] = t_mm(mixed_ref[...], grad_out_low).astype(BF16)
    grad_mixed = rounded(mm_t(grad_out_low, w_proj[...]))
    packed = packed_ref[...].astype(F32)
    attend_back(packed, grad_mixed, grad_packed_ref, edge[0], HF, windows_lon)
    grad_packed = grad_packed_ref[...].astype(BF16)
    grad_normed = rounded(mm_t(grad_packed, w_qkv[...]))
    unit, rate = norm_parts(rolled_ref[...].astype(F32))
    g_qkv[...] = t_mm((unit * gains[...]).astype(BF16), grad_packed).astype(BF16)
    grad_in, gain_sum = norm_back(grad_normed, unit, rate, gains[...])
    g_gain[...] = gain_sum
    grad_rolled = (grad_out + grad_in).astype(BF16)
    out_ref[...] = grad_rolled
    for part, pick in ((o1, s1), (o2, s2), (o3, s3)):
        part[...] = mm(pick[...], grad_rolled).astype(BF16)


def roll_kernel(own, p0, p1, p2, m0, m1, m2, m3, out):
    out[...] = gathered((own, p0, p1, p2), (m0, m1, m2, m3)).astype(BF16)


def call(body, name, operands, outs, scratch=(), scalar=False, flops=0):
    shapes = [jax.ShapeDtypeStruct(shape, dtype) for shape, dtype in outs]
    moved = sum(v.size * v.dtype.itemsize for v in operands)
    moved += sum(v.size * v.dtype.itemsize for v in shapes)
    return pl.pallas_call(
        body,
        name=name,
        out_shape=shapes,
        in_specs=[SMEM if scalar and k == 0 else VMEM for k in range(len(operands))],
        out_specs=[VMEM] * len(shapes),
        scratch_shapes=[pltpu.VMEM(shape, F32) for shape in scratch],
        compiler_params=pltpu.CompilerParams(vmem_limit_bytes=56 * 1024 * 1024),
        cost_estimate=pl.CostEstimate(flops=flops, bytes_accessed=moved, transcendentals=0),
    )(*operands)


def exchange_kernel(moves, count, *refs):
    sources, outs = refs[:count], refs[count : 2 * count]
    send_sem, recv_sem = refs[2 * count :]
    lats, lons = lax.axis_size("lat"), lax.axis_size("lon")
    lat, lon = lax.axis_index("lat"), lax.axis_index("lon")

    def at(lat_step, lon_step):
        return ((lat + lat_step + lats) % lats, (lon + lon_step + lons) % lons)

    barrier = pltpu.get_barrier_semaphore()
    for a, b in moves:
        pl.semaphore_signal(
            barrier, inc=1, device_id=at(-a, -b), device_id_type=pl.DeviceIdType.MESH
        )
    pl.semaphore_wait(barrier, len(moves))
    copies = []
    for k in range(count):
        copy = pltpu.make_async_remote_copy(
            src_ref=sources[k],
            dst_ref=outs[k],
            send_sem=send_sem.at[k],
            recv_sem=recv_sem.at[k],
            device_id=at(*moves[k % len(moves)]),
            device_id_type=pl.DeviceIdType.MESH,
        )
        copy.start()
        copies.append(copy)
    for copy in copies:
        copy.wait()


def exchange(parts, ahead, ident):
    step = -1 if ahead else 1
    moves = ((step, 0), (0, step), (step, step))
    return list(
        pl.pallas_call(
            functools.partial(exchange_kernel, moves, len(parts)),
            name=f"exchange_{ident}",
            out_shape=[jax.ShapeDtypeStruct(v.shape, v.dtype) for v in parts],
            in_specs=[VMEM] * len(parts),
            out_specs=[VMEM] * len(parts),
            scratch_shapes=[
                pltpu.SemaphoreType.DMA((len(parts),)),
                pltpu.SemaphoreType.DMA((len(parts),)),
            ],
            compiler_params=pltpu.CompilerParams(collective_id=ident, has_side_effects=True),
        )(*parts)
    )


def cut_parts(grid, ahead):
    if ahead:
        lat, lon = (slice(None, SLAT), slice(SLAT, None)), (slice(None, SLON), slice(SLON, None))
    else:
        lat = (slice(-SLAT, None), slice(None, -SLAT))
        lon = (slice(-SLON, None), slice(None, -SLON))
    picks = ((lat[0], lon[1]), (lat[1], lon[0]), (lat[0], lon[0]))
    return [grid[r, c].reshape(-1, grid.shape[2]) for r, c in picks]


def shift_pairs(lat_step, lon_step):
    lats, lons = lax.axis_size("lat"), lax.axis_size("lon")
    return [
        (a * lons + b, ((a + lat_step) % lats) * lons + (b + lon_step) % lons)
        for a in range(lats)
        for b in range(lons)
    ]


def send(value, lat_step, lon_step):
    return lax.ppermute(value, ("lat", "lon"), shift_pairs(lat_step, lon_step))


def rotate_back(grid):
    above = send(grid[-SLAT:, :-SLON], 1, 0)
    beside = send(grid[:-SLAT, -SLON:], 0, 1)
    corner = send(grid[-SLAT:, -SLON:], 1, 1)
    low = jnp.concatenate([beside, grid[:-SLAT, :-SLON]], axis=1)
    return jnp.concatenate([jnp.concatenate([corner, above], axis=1), low], axis=0)


def hop_orders():
    lons = [("lon", 1 << k) for k in range(lax.axis_size("lon").bit_length() - 1)]
    lats = [("lat", 1 << k) for k in range(lax.axis_size("lat").bit_length() - 1)]
    first, rest = lons[:1], lons[1:]
    return (
        first + rest + lats,
        first + rest[::-1] + lats,
        first + lats[:1] + rest + lats[1:],
    )


def sum_kernel(orders, *refs):
    count = len(orders)
    hops = len(orders[0])
    sources, outs = refs[:count], refs[count : 2 * count]
    lands = [refs[2 * count + c * hops : 2 * count + (c + 1) * hops] for c in range(count)]
    send_sem, recv_sem = refs[2 * count + count * hops :]
    place = {"lat": lax.axis_index("lat"), "lon": lax.axis_index("lon")}

    def bit_of(axis, step):
        return (place[axis] // step) % 2

    def partner(axis, step):
        where = dict(place)
        where[axis] = place[axis] + step - 2 * step * bit_of(axis, step)
        return (where["lat"], where["lon"])

    barrier = pltpu.get_barrier_semaphore()
    for axis, step in orders[0]:
        pl.semaphore_signal(
            barrier, inc=1, device_id=partner(axis, step), device_id_type=pl.DeviceIdType.MESH
        )
    pl.semaphore_wait(barrier, hops)

    def begin(chunk, hop):
        axis, step = orders[chunk][hop]
        source = sources[chunk] if hop == 0 else lands[chunk][hop - 1]
        half = source.shape[0] // 2
        copy = pltpu.make_async_remote_copy(
            src_ref=source.at[pl.ds((1 - bit_of(axis, step)) * half, half)],
            dst_ref=lands[chunk][hop],
            send_sem=send_sem.at[chunk, hop],
            recv_sem=recv_sem.at[chunk, hop],
            device_id=partner(axis, step),
            device_id_type=pl.DeviceIdType.MESH,
        )
        copy.start()
        return copy

    flying = [begin(chunk, 0) for chunk in range(count)]
    for hop in range(hops):
        for chunk in range(count):
            axis, step = orders[chunk][hop]
            flying[chunk].wait()
            source = sources[chunk] if hop == 0 else lands[chunk][hop - 1]
            land = lands[chunk][hop]
            half = land.shape[0]
            start = bit_of(axis, step) * half
            target = land if hop < hops - 1 else outs[chunk]

            def add(piece, carry):
                total = land[piece].astype(F32) + source[start + piece].astype(F32)
                target[piece] = total.astype(target.dtype)
                return carry

            lax.fori_loop(0, half, add, 0)
            if hop < hops - 1:
                flying[chunk] = begin(chunk, hop + 1)


def reduce_chunks(chunks):
    lats, lons = lax.axis_size("lat"), lax.axis_size("lon")
    if lats & (lats - 1) or lons & (lons - 1) or lats < 2 or lons < 2:
        return [
            lax.psum_scatter(c, ("lat", "lon"), scatter_dimension=0, tiled=True)[0].astype(F32)
            for c in chunks
        ]
    orders = hop_orders()[: len(chunks)]
    hops = len(orders[0])
    highest = [("lat", 1 << k) for k in reversed(range(lats.bit_length() - 1))]
    highest += [("lon", 1 << k) for k in reversed(range(lons.bit_length() - 1))]
    ready, lands, outs = [], [], []
    for chunk, order in zip(chunks, orders):
        tail = chunk.shape[1:]
        moved = chunk.reshape([2] * hops + list(tail))
        axes = [highest.index(bit) for bit in order] + [hops, hops + 1]
        ready.append(moved.transpose(axes).reshape(chunk.shape))
        lands += [pltpu.VMEM((1 << (hops - 1 - k),) + tail, BF16) for k in range(hops)]
        outs.append(jax.ShapeDtypeStruct((1,) + tail, F32))
    sums = pl.pallas_call(
        functools.partial(sum_kernel, orders),
        name="gradient_sums",
        out_shape=outs,
        in_specs=[VMEM] * len(ready),
        out_specs=[VMEM] * len(ready),
        scratch_shapes=lands
        + [pltpu.SemaphoreType.DMA((len(ready), hops)), pltpu.SemaphoreType.DMA((len(ready), hops))],
        compiler_params=pltpu.CompilerParams(
            collective_id=0, has_side_effects=True, vmem_limit_bytes=40 * 1024 * 1024
        ),
        cost_estimate=pl.CostEstimate(flops=10**7, bytes_accessed=10**8, transcendentals=0),
    )(*ready)
    return [value[0] for value in sums]


def as_pieces(value, devices, width):
    rows = value.shape[0] // devices
    value = value.astype(jnp.bfloat16).reshape(devices, rows, value.shape[1])
    parts = [value[:, :, i : i + width] for i in range(0, value.shape[2], width)]
    return jnp.concatenate(parts, axis=1)


def from_pieces(value, rows, columns):
    width = value.shape[1]
    parts = [value[i * rows : (i + 1) * rows] for i in range(columns // width)]
    return jnp.concatenate(parts, axis=1).astype(jnp.float32)


def local(
    tokens,
    fine_gain,
    fine_qkv,
    fine_proj,
    merge_gain,
    merge_weight,
    coarse_gain,
    coarse_qkv,
    coarse_proj,
    cotangent,
):
    fine_rows = tokens.shape[0]
    coarse_rows = fine_rows // 2
    lat_count = lax.axis_size("lat")
    lat_place = lax.axis_index("lat")
    fine_total = fine_rows * lat_count
    coarse_total = coarse_rows * lat_count
    fine_offset = lat_place * fine_rows
    coarse_offset = lat_place * coarse_rows
    grad_scale = (fine_total * tokens.shape[1] * lax.axis_size("lon") // 4) ** (-0.5)
    fine_cols, coarse_cols = tokens.shape[1], tokens.shape[1] // 2
    cells, breadth = fine_rows * fine_cols, tokens.shape[2]
    coarse_cells, coarse_breadth = cells // 4, coarse_proj.shape[1]
    fine = (fine_rows, fine_cols)
    coarse = (coarse_rows, coarse_cols)
    fine_edge = jnp.reshape(fine_total - SLAT - fine_offset, (1,)).astype(jnp.int32)
    coarse_edge = jnp.reshape(coarse_total - SLAT - coarse_offset, (1,)).astype(jnp.int32)
    sizes = [len(part) for part in roll_parts(*fine, True)]
    part_outs = [((n, breadth), BF16) for n in sizes]
    windowed, natural, merged = window_order(*fine), natural_order(*fine), merge_order(*fine)

    arrived = exchange(cut_parts(tokens, True) + cut_parts(cotangent, True), True, 1)
    arrived, cotangent_parts = arrived[:3], arrived[3:]
    inner = fine_proj.shape[0]
    rolled_fine, packed, blend, result, *parts = call(
        functools.partial(fine_forward_kernel, fine_cols // WLON),
        "fine_forward",
        [fine_edge, tokens.reshape(cells, breadth)]
        + arrived
        + assembling(*fine, True, windowed, natural)
        + sending(*fine, True, windowed)
        + [fine_gain[None], fine_qkv, fine_proj],
        [((cells, breadth), BF16), ((cells, 3 * inner), BF16), ((cells, inner), BF16)]
        + [((cells, breadth), BF16)]
        + part_outs,
        [(cells, inner)],
        True,
        3 * 10**9,
    )
    arrived = exchange(parts, True, 2)
    coarse_inner = coarse_proj.shape[0]
    coarse_windowed = window_order(*coarse)
    found = call(
        functools.partial(coarse_kernel, coarse_cols // WLON),
        "coarse",
        [coarse_edge, result]
        + arrived
        + assembling(*fine, True, merged, windowed)
        + [cotangent.reshape(coarse_cells, coarse_breadth)]
        + cotangent_parts
        + assembling(*coarse, True, coarse_windowed, natural_order(*coarse))
        + sending(*fine, False, merged)
        + [merge_gain[None], merge_weight, coarse_gain[None], coarse_qkv, coarse_proj],
        [((coarse_cells, coarse_breadth), BF16), ((cells, breadth), BF16)]
        + part_outs
        + [((1, 4 * breadth), F32), (merge_weight.shape, BF16), ((1, coarse_breadth), F32)]
        + [(coarse_qkv.shape, BF16), (coarse_proj.shape, BF16)],
        [(coarse_cells, coarse_inner), (coarse_cells, 3 * coarse_inner)],
        True,
        9 * 10**9,
    )
    coarse_result, grad_grid = found[:2]
    merge_gain_sum, merge_weight_sum, coarse_gain_sum = found[5][0], found[6], found[7][0]
    coarse_qkv_sum, coarse_proj_sum = found[8:]
    arrived = exchange(found[2:5], False, 3)
    grad_rolled, *parts = call(
        functools.partial(fine_backward_kernel, fine_cols // WLON),
        "fine_backward",
        [fine_edge, grad_grid]
        + arrived
        + assembling(*fine, False, windowed, merged)
        + sending(*fine, False, windowed)
        + [rolled_fine, packed, blend, fine_gain[None], fine_qkv, fine_proj],
        [((cells, breadth), BF16)]
        + part_outs
        + [((1, breadth), F32), (fine_qkv.shape, BF16), (fine_proj.shape, BF16)],
        [(cells, 3 * inner)],
        True,
        6 * 10**9,
    )
    fine_gain_sum, fine_qkv_sum, fine_proj_sum = parts[3][0], parts[4], parts[5]
    arrived = send_parts(parts[:3], False)
    (grad_tokens,) = call(
        roll_kernel,
        "final_roll",
        [grad_rolled] + arrived + assembling(*fine, False, natural, windowed),
        [((cells, breadth), BF16)],
        flops=10**8,
    )
    grad_tokens = grad_tokens.reshape(tokens.shape)
    coarse_grid = coarse_result.reshape(coarse_rows // WLAT, coarse_cols // WLON, WLAT, WLON, -1)
    coarse_grid = coarse_grid.transpose(0, 2, 1, 3, 4).reshape(cotangent.shape)
    output = rotate_back(coarse_grid)
    devices = lat_count * lax.axis_size("lon")

    gains = [v.reshape(devices, 1, -1) for v in (fine_gain_sum, merge_gain_sum, coarse_gain_sum)]
    gain_rows = jnp.concatenate(gains, axis=2).astype(BF16)
    gain_rows = jnp.pad(gain_rows, ((0, 0), (0, 15), (0, 256 - gain_rows.shape[2])))
    width = merge_weight.shape[1]
    mixed = [as_pieces(v, devices, 256) for v in (coarse_proj_sum, fine_qkv_sum, fine_proj_sum)]
    heights = [v.shape[1] for v in mixed]
    merge_weight_total, coarse_qkv_total, total = reduce_chunks(
        [
            as_pieces(merge_weight_sum, devices, width),
            as_pieces(coarse_qkv_sum, devices, width),
            jnp.concatenate(mixed + [gain_rows], axis=1),
        ]
    )
    merge_weight_sum = merge_weight_total
    coarse_qkv_sum = from_pieces(
        coarse_qkv_total, coarse_qkv.shape[0] // devices, coarse_qkv.shape[1]
    )
    starts = [0, heights[0], heights[0] + heights[1], sum(heights)]
    coarse_proj_sum, fine_qkv_sum, fine_proj_sum = [
        from_pieces(total[starts[k] : starts[k + 1]], w.shape[0] // devices, w.shape[1])
        for k, w in enumerate((coarse_proj, fine_qkv, fine_proj))
    ]
    first, second = gains[0].shape[2], gains[0].shape[2] + gains[1].shape[2]
    gain_sums = total[starts[3]]
    fine_gain_sum, merge_gain_sum = gain_sums[:first], gain_sums[first:second]
    coarse_gain_sum = gain_sums[second : second + gains[2].shape[2]]
    return (
        output,
        grad_tokens,
        fine_gain_sum * grad_scale,
        fine_qkv_sum * grad_scale,
        fine_proj_sum * grad_scale,
        merge_gain_sum * grad_scale,
        merge_weight_sum * grad_scale,
        coarse_gain_sum * grad_scale,
        coarse_qkv_sum * grad_scale,
        coarse_proj_sum * grad_scale,
    )


def solution(mesh):
    return jax.shard_map(
        local,
        mesh=mesh,
        in_specs=(
            P("lat", "lon", None),
            P(),
            P(),
            P(),
            P(),
            P(),
            P(),
            P(),
            P(),
            P("lat", "lon", None),
        ),
        out_specs=(
            P("lat", "lon", None),
            P("lat", "lon", None),
            P(("lat", "lon")),
            P(("lat", "lon"), None),
            P(("lat", "lon"), None),
            P(("lat", "lon")),
            P(("lat", "lon"), None),
            P(("lat", "lon")),
            P(("lat", "lon"), None),
            P(("lat", "lon"), None),
        ),
        check_vma=False,
    )
```
